32 devices in a mesh: dom: 8 (over z, x), band: 4 (over y, core).
Axes of the slice: x: 2, y: 2, z: 4, core: 2. Of those that a mesh axis runs over, the one named last changes fastest.
Arguments:
- orbitals: float32 [32, 96, 64, 128], P('band', 'dom'), may hold values from -1400 to 1400
- potential: float32 [96, 64, 128], P('dom'), may hold values from 0.1 to 2
Outputs:
- ortho_orbitals: float32 [32, 96, 64, 128], P('band', 'dom')
The draws below stay inside these ranges and needn't reach their ends.
All inputs are finite; a program needn't handle non-finite values.
Results may differ from the reference program's by a relative error of at most 0.0003.
Values sent between devices are 32-bit elements; how exact they have to be, the bound alone decides.
A program may use at most 64 MiB of HBM per device.

```python
import math
import jax
import jax.numpy as jnp
from jax import lax

NB = 32
NY = 64
NZ = 128
NX = 96


def draw_orbitals(key, part):
    key_base = jax.random.fold_in(key, 11)
    key_mix = jax.random.fold_in(key, 12)
    key_scale = jax.random.fold_in(key, 13)
    base = jnp.clip(jax.random.normal(key_base, (NB, NX, NY, NZ), jnp.float32), -6.0, 6.0)
    mixing = jnp.eye(NB, dtype=jnp.float32) + 0.7 * jnp.clip(jax.random.normal(key_mix, (NB, NB), jnp.float32), -3.0, 3.0) / math.sqrt(NB)
    scales = jnp.exp(jax.random.uniform(key_scale, (NB,), jnp.float32, 0.0, math.log(10.0)))
    mixed = jnp.einsum('ab,bxyz->axyz', mixing * scales[:, None], base, precision=lax.Precision.HIGHEST)
    rising = jnp.exp(0.6 * jnp.arange(NX, dtype=jnp.float32) / NX)
    return mixed * rising[None, :, None, None]


def shard_levels(own_key, shape, cuts, smallest, top_value):
    level = 1.0
    for position, shards_of in cuts:
        heights = jax.random.uniform(jax.random.fold_in(jax.random.fold_in(own_key, 6), position), (shards_of,), jnp.float32, smallest / len(cuts), top_value / len(cuts))
        level = level * jnp.repeat(jnp.exp(heights), shape[position] // shards_of).reshape((-1,) + (1,) * (len(shape) - 1 - position))
    return level


def setup_inputs(seed: int = 0) -> dict:
    keys = jax.random.split(jax.random.key(seed), 3)
    orbitals = draw_orbitals(jax.random.fold_in(keys[2], 71), 0)
    potential = jnp.clip(jnp.exp(math.log(2.0) - 2.9957323 * jax.random.uniform(keys[1], (NX, NY, NZ), jnp.float32) ** shard_levels(keys[1], (NX, NY, NZ), ((0, 8),), -0.2, 0.2)), 0.1, 2.0)
    return dict(orbitals=orbitals, potential=potential)


stencil_weights = [-5369.0 / 1800.0, 12.0 / 7.0, -15.0 / 56.0, 10.0 / 189.0, -1.0 / 112.0, 2.0 / 1925.0, -1.0 / 16632.0]
center_shift = 9.5
half_width = 7.5

def apply_hamiltonian(padded, field_potential):
    length = field_potential.shape[0]
    inner = padded[:, 6:6 + length]
    rows_y = inner.shape[2]
    rows_z = inner.shape[3]
    spread = jnp.pad(inner, ((0, 0), (0, 0), (6, 6), (6, 6)))
    laplace = 3.0 * stencil_weights[0] * inner
    for offset in range(1, 7):
        near = padded[:, 6 + offset:6 + offset + length] + padded[:, 6 - offset:6 - offset + length]
        near = near + spread[:, :, 6 + offset:6 + offset + rows_y, 6:6 + rows_z] + spread[:, :, 6 - offset:6 - offset + rows_y, 6:6 + rows_z]
        near = near + spread[:, :, 6:6 + rows_y, 6 + offset:6 + offset + rows_z] + spread[:, :, 6:6 + rows_y, 6 - offset:6 - offset + rows_z]
        laplace = laplace + stencil_weights[offset] * near
    return -0.5 * laplace + field_potential * inner

def reference(orbitals, potential):

    def filter_one(single):
        block = single[None]
        padded = jnp.pad(block, ((0, 0), (6, 6), (0, 0), (0, 0)))
        first = (apply_hamiltonian(padded, potential) - center_shift * block) / half_width
        padded_first = jnp.pad(first, ((0, 0), (6, 6), (0, 0), (0, 0)))
        second = 2.0 * (apply_hamiltonian(padded_first, potential) - center_shift * first) / half_width - block
        return second[0]
    filtered = lax.map(filter_one, orbitals)
    flat = filtered.reshape(NB, -1)
    correlation = jnp.dot(flat.astype(jnp.float32), flat.T.astype(jnp.float32), precision=lax.Precision.HIGHEST, preferred_element_type=jnp.float32)
    correlation = correlation / jnp.float32(NX * NY * NZ)
    lower = jnp.linalg.cholesky(correlation)
    inverse = lax.linalg.triangular_solve(lower, jnp.eye(NB, dtype=correlation.dtype), left_side=True, lower=True)
    result = jnp.dot(inverse.astype(jnp.float32), flat.astype(jnp.float32), precision=lax.Precision.HIGHEST, preferred_element_type=jnp.float32)
    return result.reshape(orbitals.shape)
```

```python
import functools
import jax
import jax.numpy as jnp
from jax import lax
from jax.experimental import pallas as pl
from jax.experimental.pallas import tpu as pltpu
from jax.sharding import PartitionSpec as P

stencil_weights = [
    -5369.0 / 1800.0,
    12.0 / 7.0,
    -15.0 / 56.0,
    10.0 / 189.0,
    -1.0 / 112.0,
    2.0 / 1925.0,
    -1.0 / 16632.0,
]
center_shift = 9.5
half_width = 7.5
reach = 6
pad = 8
scaled = [-0.5 * w / half_width for w in stencil_weights]
HIGHEST = lax.Precision.HIGHEST


def divisor(n, options):
    for c in options:
        if n % c == 0:
            return c
    return 1


def kernel(
    doms, bands, nb, nx, ny, nz,
    orb, pot, bz, out,
    u, f, filt, potb, cells, obuf, gs, ar1, ar2, inv,
    own_sem, pot_sem, swap_s, swap_r, h1_s, h1_r, h2_s, h2_r,
    a2a_s, a2a_r, a2a_l, r1_s, r1_r, r2_s, r2_r, ret_s, ret_r, ret_l,
):
    half = nb // 2
    planes = 2 * nx
    total = nb * bands
    group = 2 * bands
    slab = nx * ny
    share = slab // bands
    dom = lax.axis_index("dom")
    band = lax.axis_index("band")
    layer = dom // 2
    layers = doms // 2
    side = dom % 2
    base = layer * 2
    me = side * bands + band
    partner = {"dom": base + 1 - side, "band": band}

    def peer(j):
        g = (me + j) % group
        return g // bands, g % bands

    def peer_id(j):
        q, b = peer(j)
        return {"dom": base + q, "band": b}

    def layer_id(j):
        return {"dom": ((layer + j) % layers) * 2 + side, "band": band}

    barrier = pltpu.get_barrier_semaphore()
    for j in range(1, group):
        pl.semaphore_signal(barrier, inc=1, device_id=peer_id(j), device_id_type=pl.DeviceIdType.MESH)
    for j in range(1, layers):
        pl.semaphore_signal(barrier, inc=1, device_id=layer_id(j), device_id_type=pl.DeviceIdType.MESH)
    pl.semaphore_wait(barrier, group - 1 + layers - 1)

    def remote(src, dst, s, r, dev):
        return pltpu.make_async_remote_copy(
            src_ref=src, dst_ref=dst, send_sem=s, recv_sem=r,
            device_id=dev, device_id_type=pl.DeviceIdType.MESH,
        )

    rows = pl.ds(pad, ny)
    mine = pl.ds(reach + side * nx, nx)

    def swap(o):
        return remote(
            orb.at[(1 - side) * half + o], u.at[o, mine, rows], swap_s.at[o], swap_r.at[o], partner
        )

    swap_pot = remote(pot, potb.at[pl.ds(side * nx, nx)], swap_s.at[half], swap_r.at[half], partner)

    def own(o):
        return pltpu.make_async_copy(orb.at[side * half + o], u.at[o, mine, rows], own_sem.at[o])

    own_pot = pltpu.make_async_copy(pot, potb.at[pl.ds(side * nx, nx)], pot_sem)

    swap(0).start()
    swap_pot.start()
    for o in range(1, half):
        swap(o).start()
    for o in range(half):
        own(o).start()
    own_pot.start()

    def up(buf, o, s, r):
        return remote(
            buf.at[o, pl.ds(planes, reach), rows], buf.at[o, pl.ds(0, reach), rows],
            s.at[0, o], r.at[0, o], {"dom": dom + 2, "band": band},
        )

    def down(buf, o, s, r):
        return remote(
            buf.at[o, pl.ds(reach, reach), rows], buf.at[o, pl.ds(planes + reach, reach), rows],
            s.at[1, o], r.at[1, o], {"dom": dom - 2, "band": band},
        )

    has_up = layer < layers - 1
    has_down = layer > 0

    def send_halos(buf, o, s, r):
        @pl.when(has_up)
        def _():
            up(buf, o, s, r).start()

        @pl.when(has_down)
        def _():
            down(buf, o, s, r).start()

    def wait_halos(buf, o, s, r):
        @pl.when(has_down)
        def _():
            up(buf, o, s, r).wait_recv()

        @pl.when(has_up)
        def _():
            down(buf, o, s, r).wait_recv()

    edge = jnp.zeros((planes + 2 * reach, pad, nz), jnp.float32)
    for buf in (u, f):
        for o in range(half):
            buf[o, :, pl.ds(0, pad), :] = edge
            buf[o, :, pl.ds(pad + ny, pad), :] = edge
    empty = jnp.zeros((reach, ny, nz), jnp.float32)
    for buf in (u, f):
        for o in range(half):
            @pl.when(jnp.logical_not(has_down))
            def _():
                buf[o, pl.ds(0, reach), rows, :] = empty

            @pl.when(jnp.logical_not(has_up))
            def _():
                buf[o, pl.ds(planes + reach, reach), rows, :] = empty

    step = divisor(planes, (4, 3, 2))

    def apply(buf, o, emit):
        def body(t, carry):
            x0 = t * step
            centre = [buf[o, reach + x0 + i, pl.ds(pad, ny), :] for i in range(step)]
            along_z = jnp.dot(
                jnp.concatenate(centre, axis=0), bz[...], precision=HIGHEST,
                preferred_element_type=jnp.float32,
            )
            for i in range(step):
                x = reach + x0 + i
                weight = potb[x0 + i] * (1.0 / half_width) + (
                    3.0 * scaled[0] - center_shift / half_width
                )
                acc = along_z[i * ny:(i + 1) * ny] + weight * centre[i]
                for k in range(1, reach + 1):
                    near = buf[o, x + k, pl.ds(pad, ny), :] + buf[o, x - k, pl.ds(pad, ny), :]
                    near = near + (
                        buf[o, x, pl.ds(pad + k, ny), :] + buf[o, x, pl.ds(pad - k, ny), :]
                    )
                    acc = acc + scaled[k] * near
                emit(x0 + i, acc)
            return carry

        lax.fori_loop(0, planes // step, body, 0)

    def stage_a(o):
        own(o).wait()
        swap(o).wait_recv()
        send_halos(u, o, h1_s, h1_r)

    def stage_b(o):
        wait_halos(u, o, h1_s, h1_r)

        def emit(x, acc):
            f[o, reach + x, pl.ds(pad, ny), :] = acc

        apply(u, o, emit)
        send_halos(f, o, h2_s, h2_r)

    def a2a(o, j):
        q, b = peer(j)
        first = pl.multiple_of(q * slab + b * share, 8)
        to = pl.multiple_of((band * nb + side * half + o) * share, 8)
        return remote(
            filt.at[o, pl.ds(first, share)], cells.at[pl.ds(to, share)],
            a2a_s.at[j - 1, o], a2a_r.at[j - 1, o], peer_id(j),
        )

    def a2a_own(o):
        first = pl.multiple_of(me * share, 8)
        to = pl.multiple_of((band * nb + side * half + o) * share, 8)
        return pltpu.make_async_copy(
            filt.at[o, pl.ds(first, share)], cells.at[pl.ds(to, share)], a2a_l.at[o]
        )

    def stage_c(o):
        wait_halos(f, o, h2_s, h2_r)

        def emit(x, acc):
            start = pl.multiple_of(x * ny, 8)
            filt[o, pl.ds(start, ny), :] = 2.0 * acc - u[o, reach + x, pl.ds(pad, ny), :]

        apply(f, o, emit)
        for j in range(1, group):
            a2a(o, j).start()
        a2a_own(o).start()

    stage_a(0)
    own_pot.wait()
    swap_pot.wait_recv()
    stage_b(0)
    for o in range(1, half):
        stage_a(o)
        stage_c(o - 1)
        stage_b(o)
    stage_c(half - 1)

    for o in range(half):
        a2a_own(o).wait()
        for j in range(1, group):
            a2a(o, j).wait_recv()

    chunk = divisor(share, (16, 8))

    def gather(t):
        return jnp.concatenate(
            [cells[pl.ds(t * chunk + i, total, stride=share), :] for i in range(chunk)], axis=1
        )

    def gram_body(t, acc):
        x = gather(t)
        return acc + lax.dot_general(
            x, x, (((1,), (1,)), ((), ())), precision=HIGHEST, preferred_element_type=jnp.float32
        )

    gram = lax.fori_loop(0, share // chunk, gram_body, jnp.zeros((total, total), jnp.float32))
    gs[...] = jnp.zeros_like(gs)
    gs[0, :, pl.ds(0, total)] = gram
    ar1[me] = gs[0]

    def reduce_1(j):
        return remote(gs.at[0], ar1.at[me], r1_s.at[j - 1], r1_r.at[j - 1], peer_id(j))

    def reduce_2(j):
        return remote(gs.at[1], ar2.at[layer], r2_s.at[j - 1], r2_r.at[j - 1], layer_id(j))

    for j in range(1, group):
        reduce_1(j).start()
    for j in range(1, group):
        reduce_1(j).wait_recv()
    part = ar1[0]
    for j in range(1, group):
        part = part + ar1[j]
    gs[1] = part
    ar2[layer] = part
    for j in range(1, layers):
        reduce_2(j).start()
    for j in range(1, layers):
        reduce_2(j).wait_recv()
    work = ar2[0]
    for j in range(1, layers):
        work = work + ar2[j]

    lane = lax.broadcasted_iota(jnp.int32, work.shape, 1)
    row = lax.broadcasted_iota(jnp.int32, work.shape, 0)
    work = work / jnp.float32(slab * doms * nz)
    work = jnp.where(lane == row + total, jnp.float32(1.0), work)
    for k in range(total):
        root = jnp.sqrt(work[k:k + 1, k:k + 1])
        scale = 1.0 / root
        pivot = work[k:k + 1, :] * scale
        column = work[:, k:k + 1] * scale
        work = jnp.where(row > k, work - column * pivot, jnp.where(row == k, pivot, work))
    inv[...] = work[:, total:2 * total]

    pieces = divisor(share // chunk, (4, 3, 2))
    piece = share // pieces
    obuf3 = obuf.reshape(total, share, nz)

    def ret(s, j):
        b = (band + j) % bands
        at = pl.multiple_of(band * share + s * piece, 8)
        return remote(
            obuf3.at[pl.ds(b * nb, nb), pl.ds(s * piece, piece)],
            out.at[:, pl.ds(at, piece)],
            ret_s.at[j - 1, s], ret_r.at[j - 1, s], {"dom": dom, "band": b},
        )

    def ret_own(s):
        at = pl.multiple_of(band * share + s * piece, 8)
        return pltpu.make_async_copy(
            obuf3.at[pl.ds(band * nb, nb), pl.ds(s * piece, piece)],
            out.at[:, pl.ds(at, piece)], ret_l.at[s],
        )

    for s in range(pieces):
        def ortho_body(t, carry):
            y = jnp.dot(inv[...], gather(t), precision=HIGHEST, preferred_element_type=jnp.float32)
            for i in range(chunk):
                obuf[pl.ds(t * chunk + i, total, stride=share), :] = y[:, i * nz:(i + 1) * nz]
            return carry

        lax.fori_loop(s * (piece // chunk), (s + 1) * (piece // chunk), ortho_body, 0)
        for j in range(1, bands):
            ret(s, j).start()
        ret_own(s).start()

    swap_pot.wait_send()
    for o in range(half):
        swap(o).wait_send()

        @pl.when(has_up)
        def _():
            up(u, o, h1_s, h1_r).wait_send()
            up(f, o, h2_s, h2_r).wait_send()

        @pl.when(has_down)
        def _():
            down(u, o, h1_s, h1_r).wait_send()
            down(f, o, h2_s, h2_r).wait_send()

        for j in range(1, group):
            a2a(o, j).wait_send()
    for j in range(1, group):
        reduce_1(j).wait_send()
    for j in range(1, layers):
        reduce_2(j).wait_send()
    for s in range(pieces):
        ret_own(s).wait()
        for j in range(1, bands):
            ret(s, j).wait()


def shards(doms, bands, orbitals, potential):
    nb, nx, ny, nz = orbitals.shape
    half = nb // 2
    total = nb * bands
    group = 2 * bands
    layers = doms // 2
    slab = nx * ny
    share = slab // bands
    distance = jnp.abs(
        lax.broadcasted_iota(jnp.int32, (nz, nz), 0) - lax.broadcasted_iota(jnp.int32, (nz, nz), 1)
    )
    bz = jnp.zeros((nz, nz), jnp.float32)
    for k in range(1, reach + 1):
        bz = jnp.where(distance == k, jnp.float32(scaled[k]), bz)
    dma = pltpu.SemaphoreType.DMA
    f32 = jnp.float32
    wide = max(nz, 2 * total)
    pieces = divisor(share // divisor(share, (16, 8)), (4, 3, 2))
    out = pl.pallas_call(
        functools.partial(kernel, doms, bands, nb, nx, ny, nz),
        out_shape=jax.ShapeDtypeStruct((nb, slab, nz), f32),
        in_specs=[
            pl.BlockSpec(memory_space=pl.ANY),
            pl.BlockSpec(memory_space=pl.ANY),
            pl.BlockSpec(memory_space=pltpu.VMEM),
        ],
        out_specs=pl.BlockSpec(memory_space=pl.ANY),
        scratch_shapes=[
            pltpu.VMEM((half, 2 * nx + 2 * reach, ny + 2 * pad, nz), f32),
            pltpu.VMEM((half, 2 * nx + 2 * reach, ny + 2 * pad, nz), f32),
            pltpu.VMEM((half, 2 * slab, nz), f32),
            pltpu.VMEM((2 * nx, ny, nz), f32),
            pltpu.VMEM((total * share, nz), f32),
            pltpu.VMEM((total * share, nz), f32),
            pltpu.VMEM((2, total, wide), f32),
            pltpu.VMEM((group, total, wide), f32),
            pltpu.VMEM((layers, total, wide), f32),
            pltpu.VMEM((total, total), f32),
            dma((half,)),
            dma,
            dma((half + 1,)),
            dma((half + 1,)),
            dma((2, half)),
            dma((2, half)),
            dma((2, half)),
            dma((2, half)),
            dma((group - 1, half)),
            dma((group - 1, half)),
            dma((half,)),
            dma((group - 1,)),
            dma((group - 1,)),
            dma((max(layers - 1, 1),)),
            dma((max(layers - 1, 1),)),
            dma((max(bands - 1, 1), pieces)),
            dma((max(bands - 1, 1), pieces)),
            dma((pieces,)),
        ],
        compiler_params=pltpu.CompilerParams(
            collective_id=0, has_side_effects=True, vmem_limit_bytes=56 * 1024 * 1024
        ),
    )(orbitals, potential, bz)
    return out.reshape(orbitals.shape)


def solution(mesh):
    in_specs = (P("band", "dom", None, None), P("dom", None, None))
    out_specs = P("band", "dom", None, None)
    body = functools.partial(shards, mesh.shape["dom"], mesh.shape["band"])
    return jax.shard_map(body, mesh=mesh, in_specs=in_specs, out_specs=out_specs, check_vma=False)
```

```python
import functools
import jax
import jax.numpy as jnp
from jax import lax
from jax.experimental import pallas as pl
from jax.experimental.pallas import tpu as pltpu
from jax.sharding import PartitionSpec as P

stencil_weights = [
    -5369.0 / 1800.0,
    12.0 / 7.0,
    -15.0 / 56.0,
    10.0 / 189.0,
    -1.0 / 112.0,
    2.0 / 1925.0,
    -1.0 / 16632.0,
]
center_shift = 9.5
half_width = 7.5
reach = 6
pad = 8
scaled = [-0.5 * w / half_width for w in stencil_weights]
HIGHEST = lax.Precision.HIGHEST


def divisor(n, options):
    for c in options:
        if n % c == 0:
            return c
    return 1


def packed_rows(total, nz):
    fold = nz // total if total < nz and nz % total == 0 else 1
    return total // fold if total % (8 * fold) == 0 else total


def kernel(
    doms, bands, nb, nx, ny, nz,
    orb, pot, out,
    bz, u, f, filt, potb, cells, obuf, gs, ar1, ar2, inv,
    own_sem, pot_sem, pot_s, pot_r, swap_s, swap_r, h1_s, h1_r, h2_s, h2_r,
    a2a_s, a2a_r, a2a_l, r1_s, r1_r, r2_s, r2_r, ret_s, ret_r, ret_l,
):
    half = nb // 2
    planes = 2 * nx
    total = nb * bands
    group = 2 * bands
    slab = nx * ny
    share = slab // bands
    dom = lax.axis_index("dom")
    band = lax.axis_index("band")
    layer = dom // 2
    layers = doms // 2
    side = dom % 2
    base = layer * 2
    me = side * bands + band
    partner = {"dom": base + 1 - side, "band": band}

    def peer(j):
        g = (me + j) % group
        return g // bands, g % bands

    def peer_id(j):
        q, b = peer(j)
        return {"dom": base + q, "band": b}

    def layer_id(j):
        return {"dom": ((layer + j) % layers) * 2 + side, "band": band}

    barrier = pltpu.get_barrier_semaphore()
    for j in range(1, group):
        pl.semaphore_signal(barrier, inc=1, device_id=peer_id(j), device_id_type=pl.DeviceIdType.MESH)
    for j in range(1, layers):
        pl.semaphore_signal(barrier, inc=1, device_id=layer_id(j), device_id_type=pl.DeviceIdType.MESH)
    pl.semaphore_wait(barrier, group - 1 + layers - 1)

    def remote(src, dst, s, r, dev):
        return pltpu.make_async_remote_copy(
            src_ref=src, dst_ref=dst, send_sem=s, recv_sem=r,
            device_id=dev, device_id_type=pl.DeviceIdType.MESH,
        )

    rows = pl.ds(pad, ny)
    mine = pl.ds(reach + side * nx, nx)

    def swap(o):
        return remote(
            orb.at[(1 - side) * half + o], u.at[o, mine, rows], swap_s.at[o], swap_r.at[o], partner
        )

    pot_rows = pl.ds(pl.multiple_of(band * share, 8), share)
    my_pot = pl.ds(pl.multiple_of(side * slab + band * share, 8), share)
    got_pot = pl.ds(pl.multiple_of((1 - side) * slab + band * share, 8), share)
    swap_pot = remote(pot.at[pot_rows], potb.at[my_pot], pot_s.at[0], pot_r.at[0], partner)

    def pass_pot(j):
        return remote(
            potb.at[got_pot], potb.at[got_pot], pot_s.at[j], pot_r.at[j],
            {"dom": dom, "band": (band + j) % bands},
        )

    def own(o):
        return pltpu.make_async_copy(orb.at[side * half + o], u.at[o, mine, rows], own_sem.at[o])

    own_pot = pltpu.make_async_copy(
        pot, potb.at[pl.ds(pl.multiple_of(side * slab, 8), slab)], pot_sem
    )

    swap(0).start()
    swap_pot.start()
    for o in range(1, half):
        swap(o).start()
    for o in range(half):
        own(o).start()
    own_pot.start()

    def up(buf, o, s, r):
        return remote(
            buf.at[o, pl.ds(planes, reach), rows], buf.at[o, pl.ds(0, reach), rows],
            s.at[0, o], r.at[0, o], {"dom": dom + 2, "band": band},
        )

    def down(buf, o, s, r):
        return remote(
            buf.at[o, pl.ds(reach, reach), rows], buf.at[o, pl.ds(planes + reach, reach), rows],
            s.at[1, o], r.at[1, o], {"dom": dom - 2, "band": band},
        )

    has_up = layer < layers - 1
    has_down = layer > 0

    def send_halos(buf, o, s, r):
        @pl.when(has_up)
        def _():
            up(buf, o, s, r).start()

        @pl.when(has_down)
        def _():
            down(buf, o, s, r).start()

    def wait_halos(buf, o, s, r):
        @pl.when(has_down)
        def _():
            up(buf, o, s, r).wait_recv()

        @pl.when(has_up)
        def _():
            down(buf, o, s, r).wait_recv()

    distance = jnp.abs(
        lax.broadcasted_iota(jnp.int32, (nz, nz), 0) - lax.broadcasted_iota(jnp.int32, (nz, nz), 1)
    )
    banded = jnp.zeros((nz, nz), jnp.float32)
    for k in range(1, reach + 1):
        banded = jnp.where(distance == k, jnp.float32(scaled[k]), banded)
    bz[...] = banded
    edge = jnp.zeros((planes + 2 * reach, pad, nz), jnp.float32)
    for buf in (u, f):
        for o in range(half):
            buf[o, :, pl.ds(0, pad), :] = edge
            buf[o, :, pl.ds(pad + ny, pad), :] = edge
    empty = jnp.zeros((reach, ny, nz), jnp.float32)
    for buf in (u, f):
        for o in range(half):
            @pl.when(jnp.logical_not(has_down))
            def _():
                buf[o, pl.ds(0, reach), rows, :] = empty

            @pl.when(jnp.logical_not(has_up))
            def _():
                buf[o, pl.ds(planes + reach, reach), rows, :] = empty

    step = divisor(planes, (4, 3, 2))

    def apply(buf, o, emit):
        def body(t, carry):
            x0 = t * step
            centre = [buf[o, reach + x0 + i, pl.ds(pad, ny), :] for i in range(step)]
            along_z = jnp.dot(
                jnp.concatenate(centre, axis=0), bz[...], precision=HIGHEST,
                preferred_element_type=jnp.float32,
            )
            for i in range(step):
                x = reach + x0 + i
                weight = potb[pl.ds(pl.multiple_of((x0 + i) * ny, 8), ny), :] * (1.0 / half_width) + (
                    3.0 * scaled[0] - center_shift / half_width
                )
                acc = along_z[i * ny:(i + 1) * ny] + weight * centre[i]
                for k in range(1, reach + 1):
                    near = buf[o, x + k, pl.ds(pad, ny), :] + buf[o, x - k, pl.ds(pad, ny), :]
                    near = near + (
                        buf[o, x, pl.ds(pad + k, ny), :] + buf[o, x, pl.ds(pad - k, ny), :]
                    )
                    acc = acc + scaled[k] * near
                emit(x0 + i, acc)
            return carry

        lax.fori_loop(0, planes // step, body, 0)

    def stage_a(o):
        own(o).wait()
        swap(o).wait_recv()
        send_halos(u, o, h1_s, h1_r)

    def stage_b(o):
        wait_halos(u, o, h1_s, h1_r)

        def emit(x, acc):
            f[o, reach + x, pl.ds(pad, ny), :] = acc

        apply(u, o, emit)
        send_halos(f, o, h2_s, h2_r)

    def a2a(o, j):
        q, b = peer(j)
        first = pl.multiple_of(q * slab + b * share, 8)
        to = pl.multiple_of((band * nb + side * half + o) * share, 8)
        return remote(
            filt.at[o, pl.ds(first, share)], cells.at[pl.ds(to, share)],
            a2a_s.at[j - 1, o], a2a_r.at[j - 1, o], peer_id(j),
        )

    def a2a_own(o):
        first = pl.multiple_of(me * share, 8)
        to = pl.multiple_of((band * nb + side * half + o) * share, 8)
        return pltpu.make_async_copy(
            filt.at[o, pl.ds(first, share)], cells.at[pl.ds(to, share)], a2a_l.at[o]
        )

    def stage_c(o):
        wait_halos(f, o, h2_s, h2_r)

        def emit(x, acc):
            start = pl.multiple_of(x * ny, 8)
            filt[o, pl.ds(start, ny), :] = 2.0 * acc - u[o, reach + x, pl.ds(pad, ny), :]

        apply(f, o, emit)
        for j in range(1, group):
            a2a(o, j).start()
        a2a_own(o).start()

    stage_a(0)
    own_pot.wait()
    swap_pot.wait_recv()
    for j in range(1, bands):
        pass_pot(j).start()
    for j in range(1, bands):
        pass_pot(j).wait_recv()
    stage_b(0)
    for o in range(1, half):
        stage_a(o)
        stage_c(o - 1)
        stage_b(o)
    stage_c(half - 1)

    for o in range(half):
        a2a_own(o).wait()
        for j in range(1, group):
            a2a(o, j).wait_recv()

    packed = packed_rows(total, nz)
    chunk = divisor(share, (16, 8))

    def gather(t):
        return jnp.concatenate(
            [cells[pl.ds(t * chunk + i, total, stride=share), :] for i in range(chunk)], axis=1
        )

    def gram_body(t, acc):
        x = gather(t)
        return acc + lax.dot_general(
            x, x, (((1,), (1,)), ((), ())), precision=HIGHEST, preferred_element_type=jnp.float32
        )

    gram = lax.fori_loop(0, share // chunk, gram_body, jnp.zeros((total, total), jnp.float32))
    gram = jnp.concatenate(
        [gram[i * packed:(i + 1) * packed] for i in range(total // packed)], axis=1
    )
    gs[0] = gram
    ar1[me] = gram

    def reduce_1(j):
        return remote(gs.at[0], ar1.at[me], r1_s.at[j - 1], r1_r.at[j - 1], peer_id(j))

    def reduce_2(j):
        return remote(gs.at[1], ar2.at[layer], r2_s.at[j - 1], r2_r.at[j - 1], layer_id(j))

    for j in range(1, group):
        reduce_1(j).start()
    for j in range(1, group):
        reduce_1(j).wait_recv()
    part = ar1[0]
    for j in range(1, group):
        part = part + ar1[j]
    gs[1] = part
    ar2[layer] = part
    for j in range(1, layers):
        reduce_2(j).start()
    for j in range(1, layers):
        reduce_2(j).wait_recv()
    work = ar2[0]
    for j in range(1, layers):
        work = work + ar2[j]

    work = jnp.concatenate(
        [work[:, i * total:(i + 1) * total] for i in range(total // packed)], axis=0
    )
    work = jnp.concatenate([work, jnp.zeros((total, total), jnp.float32)], axis=1)
    lane = lax.broadcasted_iota(jnp.int32, work.shape, 1)
    row = lax.broadcasted_iota(jnp.int32, work.shape, 0)
    work = work / jnp.float32(slab * doms * nz)
    work = jnp.where(lane == row + total, jnp.float32(1.0), work)
    for k in range(total):
        root = jnp.sqrt(work[k:k + 1, k:k + 1])
        scale = 1.0 / root
        pivot = work[k:k + 1, :] * scale
        column = work[:, k:k + 1] * scale
        work = jnp.where(row > k, work - column * pivot, jnp.where(row == k, pivot, work))
    inv[...] = work[:, total:2 * total]

    pieces = divisor(share // chunk, (4, 3, 2))
    piece = share // pieces
    obuf3 = obuf.reshape(total, share, nz)

    def ret(s, j):
        b = (band + j) % bands
        at = pl.multiple_of(band * share + s * piece, 8)
        return remote(
            obuf3.at[pl.ds(b * nb, nb), pl.ds(s * piece, piece)],
            out.at[:, pl.ds(at, piece)],
            ret_s.at[j - 1, s], ret_r.at[j - 1, s], {"dom": dom, "band": b},
        )

    def ret_own(s):
        at = pl.multiple_of(band * share + s * piece, 8)
        return pltpu.make_async_copy(
            obuf3.at[pl.ds(band * nb, nb), pl.ds(s * piece, piece)],
            out.at[:, pl.ds(at, piece)], ret_l.at[s],
        )

    for s in range(pieces):
        def ortho_body(t, carry):
            y = jnp.dot(inv[...], gather(t), precision=HIGHEST, preferred_element_type=jnp.float32)
            for i in range(chunk):
                obuf[pl.ds(t * chunk + i, total, stride=share), :] = y[:, i * nz:(i + 1) * nz]
            return carry

        lax.fori_loop(s * (piece // chunk), (s + 1) * (piece // chunk), ortho_body, 0)
        for j in range(1, bands):
            ret(s, j).start()
        ret_own(s).start()

    swap_pot.wait_send()
    for j in range(1, bands):
        pass_pot(j).wait_send()
    for o in range(half):
        swap(o).wait_send()

        @pl.when(has_up)
        def _():
            up(u, o, h1_s, h1_r).wait_send()
            up(f, o, h2_s, h2_r).wait_send()

        @pl.when(has_down)
        def _():
            down(u, o, h1_s, h1_r).wait_send()
            down(f, o, h2_s, h2_r).wait_send()

        for j in range(1, group):
            a2a(o, j).wait_send()
    for j in range(1, group):
        reduce_1(j).wait_send()
    for j in range(1, layers):
        reduce_2(j).wait_send()
    for s in range(pieces):
        ret_own(s).wait()
        for j in range(1, bands):
            ret(s, j).wait()


def deliver(held, out, sem):
    copy = pltpu.make_async_copy(held, out, sem)
    copy.start()
    copy.wait()


def shards(doms, bands, orbitals, potential):
    nb, nx, ny, nz = orbitals.shape
    half = nb // 2
    total = nb * bands
    group = 2 * bands
    layers = doms // 2
    slab = nx * ny
    share = slab // bands
    dma = pltpu.SemaphoreType.DMA
    f32 = jnp.float32
    packed = packed_rows(total, nz)
    wide = total * total // packed
    pieces = divisor(share // divisor(share, (16, 8)), (4, 3, 2))
    out = pl.pallas_call(
        functools.partial(kernel, doms, bands, nb, nx, ny, nz),
        out_shape=pltpu.VMEM((nb, slab, nz), f32),
        in_specs=[
            pl.BlockSpec(memory_space=pl.ANY),
            pl.BlockSpec(memory_space=pl.ANY),
        ],
        out_specs=pl.BlockSpec(memory_space=pltpu.VMEM),
        scratch_shapes=[
            pltpu.VMEM((nz, nz), f32),
            pltpu.VMEM((half, 2 * nx + 2 * reach, ny + 2 * pad, nz), f32),
            pltpu.VMEM((half, 2 * nx + 2 * reach, ny + 2 * pad, nz), f32),
            pltpu.VMEM((half, 2 * slab, nz), f32),
            pltpu.VMEM((2 * slab, nz), f32),
            pltpu.VMEM((total * share, nz), f32),
            pltpu.VMEM((total * share, nz), f32),
            pltpu.VMEM((2, packed, wide), f32),
            pltpu.VMEM((group, packed, wide), f32),
            pltpu.VMEM((layers, packed, wide), f32),
            pltpu.VMEM((total, total), f32),
            dma((half,)),
            dma,
            dma((bands,)),
            dma((bands,)),
            dma((half,)),
            dma((half,)),
            dma((2, half)),
            dma((2, half)),
            dma((2, half)),
            dma((2, half)),
            dma((group - 1, half)),
            dma((group - 1, half)),
            dma((half,)),
            dma((group - 1,)),
            dma((group - 1,)),
            dma((max(layers - 1, 1),)),
            dma((max(layers - 1, 1),)),
            dma((max(bands - 1, 1), pieces)),
            dma((max(bands - 1, 1), pieces)),
            dma((pieces,)),
        ],
        compiler_params=pltpu.CompilerParams(
            collective_id=0, has_side_effects=True, vmem_limit_bytes=60 * 1024 * 1024
        ),
    )(orbitals, potential.reshape(slab, nz))
    out = pl.pallas_call(
        deliver,
        out_shape=jax.ShapeDtypeStruct((nb, slab, nz), f32),
        in_specs=[pl.BlockSpec(memory_space=pltpu.VMEM)],
        out_specs=pl.BlockSpec(memory_space=pl.ANY),
        scratch_shapes=[dma],
    )(out)
    return out.reshape(orbitals.shape)


def solution(mesh):
    in_specs = (P("band", "dom", None, None), P("dom", None, None))
    out_specs = P("band", "dom", None, None)
    body = functools.partial(shards, mesh.shape["dom"], mesh.shape["band"])
    return jax.shard_map(body, mesh=mesh, in_specs=in_specs, out_specs=out_specs, check_vma=False)
```

```python
import functools
import jax
import jax.numpy as jnp
from jax import lax
from jax.experimental import pallas as pl
from jax.experimental.pallas import tpu as pltpu
from jax.sharding import PartitionSpec as P

stencil_weights = [
    -5369.0 / 1800.0,
    12.0 / 7.0,
    -15.0 / 56.0,
    10.0 / 189.0,
    -1.0 / 112.0,
    2.0 / 1925.0,
    -1.0 / 16632.0,
]
center_shift = 9.5
half_width = 7.5
reach = 6
pad = 8
scaled = [-0.5 * w / half_width for w in stencil_weights]
HIGHEST = lax.Precision.HIGHEST


def divisor(n, options):
    for c in options:
        if n % c == 0:
            return c
    return 1


def packed_rows(total, nz):
    fold = nz // total if total < nz and nz % total == 0 else 1
    return total // fold if total % (8 * fold) == 0 else total


def kernel(
    doms, bands, nb, nx, ny, nz,
    orb, pot, full, coef,
    bz, u, f, filt, potb, cells, gs, ar1, ar2,
    own_sem, pot_sem, pot_s, pot_r, swap_s, swap_r, h1_s, h1_r, h2_s, h2_r,
    out_s, out_r, gram_s, gram_r, gram_l, rest_s, rest_r, pass_s, pass_r, mate_s, mate_r, keep_l,
    r1_s, r1_r, r2_s, r2_r,
):
    half = nb // 2
    planes = 2 * nx
    total = nb * bands
    group = 2 * bands
    slab = nx * ny
    share = slab // bands
    dom = lax.axis_index("dom")
    band = lax.axis_index("band")
    layer = dom // 2
    layers = doms // 2
    side = dom % 2
    base = layer * 2
    me = side * bands + band
    partner = {"dom": base + 1 - side, "band": band}

    def peer(j):
        g = (me + j) % group
        return g // bands, g % bands

    def peer_id(j):
        q, b = peer(j)
        return {"dom": base + q, "band": b}

    def layer_id(j):
        return {"dom": ((layer + j) % layers) * 2 + side, "band": band}

    barrier = pltpu.get_barrier_semaphore()
    for j in range(1, group):
        pl.semaphore_signal(barrier, inc=1, device_id=peer_id(j), device_id_type=pl.DeviceIdType.MESH)
    for j in range(1, layers):
        pl.semaphore_signal(barrier, inc=1, device_id=layer_id(j), device_id_type=pl.DeviceIdType.MESH)
    pl.semaphore_wait(barrier, group - 1 + layers - 1)

    def remote(src, dst, s, r, dev):
        return pltpu.make_async_remote_copy(
            src_ref=src, dst_ref=dst, send_sem=s, recv_sem=r,
            device_id=dev, device_id_type=pl.DeviceIdType.MESH,
        )

    rows = pl.ds(pad, ny)
    mine = pl.ds(reach + side * nx, nx)

    def swap(o):
        return remote(
            orb.at[(1 - side) * half + o], u.at[o, mine, rows], swap_s.at[o], swap_r.at[o], partner
        )

    pot_rows = pl.ds(pl.multiple_of(band * share, 8), share)
    my_pot = pl.ds(pl.multiple_of(side * slab + band * share, 8), share)
    got_pot = pl.ds(pl.multiple_of((1 - side) * slab + band * share, 8), share)
    swap_pot = remote(pot.at[pot_rows], potb.at[my_pot], pot_s.at[0], pot_r.at[0], partner)

    def pass_pot(j):
        return remote(
            potb.at[got_pot], potb.at[got_pot], pot_s.at[j], pot_r.at[j],
            {"dom": dom, "band": (band + j) % bands},
        )

    def own(o):
        return pltpu.make_async_copy(orb.at[side * half + o], u.at[o, mine, rows], own_sem.at[o])

    own_pot = pltpu.make_async_copy(
        pot, potb.at[pl.ds(pl.multiple_of(side * slab, 8), slab)], pot_sem
    )

    swap(0).start()
    swap_pot.start()
    for o in range(1, half):
        swap(o).start()
    for o in range(half):
        own(o).start()
    own_pot.start()

    def up(buf, o, s, r):
        return remote(
            buf.at[o, pl.ds(planes, reach), rows], buf.at[o, pl.ds(0, reach), rows],
            s.at[0, o], r.at[0, o], {"dom": dom + 2, "band": band},
        )

    def down(buf, o, s, r):
        return remote(
            buf.at[o, pl.ds(reach, reach), rows], buf.at[o, pl.ds(planes + reach, reach), rows],
            s.at[1, o], r.at[1, o], {"dom": dom - 2, "band": band},
        )

    has_up = layer < layers - 1
    has_down = layer > 0

    def send_halos(buf, o, s, r):
        @pl.when(has_up)
        def _():
            up(buf, o, s, r).start()

        @pl.when(has_down)
        def _():
            down(buf, o, s, r).start()

    def wait_halos(buf, o, s, r):
        @pl.when(has_down)
        def _():
            up(buf, o, s, r).wait_recv()

        @pl.when(has_up)
        def _():
            down(buf, o, s, r).wait_recv()

    distance = jnp.abs(
        lax.broadcasted_iota(jnp.int32, (nz, nz), 0) - lax.broadcasted_iota(jnp.int32, (nz, nz), 1)
    )
    banded = jnp.zeros((nz, nz), jnp.float32)
    for k in range(1, reach + 1):
        banded = jnp.where(distance == k, jnp.float32(scaled[k]), banded)
    bz[...] = banded
    edge = jnp.zeros((planes + 2 * reach, pad, nz), jnp.float32)
    for buf in (u, f):
        for o in range(half):
            buf[o, :, pl.ds(0, pad), :] = edge
            buf[o, :, pl.ds(pad + ny, pad), :] = edge
    empty = jnp.zeros((reach, ny, nz), jnp.float32)
    for buf in (u, f):
        for o in range(half):
            @pl.when(jnp.logical_not(has_down))
            def _():
                buf[o, pl.ds(0, reach), rows, :] = empty

            @pl.when(jnp.logical_not(has_up))
            def _():
                buf[o, pl.ds(planes + reach, reach), rows, :] = empty

    step = divisor(nx, (4, 3, 2))

    def apply(buf, o, emit, low, count):
        def body(t, carry):
            x0 = low + t * step
            centre = [buf[o, reach + x0 + i, pl.ds(pad, ny), :] for i in range(step)]
            along_z = jnp.dot(
                jnp.concatenate(centre, axis=0), bz[...], precision=HIGHEST,
                preferred_element_type=jnp.float32,
            )
            for i in range(step):
                x = reach + x0 + i
                weight = potb[pl.ds(pl.multiple_of((x0 + i) * ny, 8), ny), :] * (1.0 / half_width) + (
                    3.0 * scaled[0] - center_shift / half_width
                )
                acc = along_z[i * ny:(i + 1) * ny] + weight * centre[i]
                for k in range(1, reach + 1):
                    near = buf[o, x + k, pl.ds(pad, ny), :] + buf[o, x - k, pl.ds(pad, ny), :]
                    near = near + (
                        buf[o, x, pl.ds(pad + k, ny), :] + buf[o, x, pl.ds(pad - k, ny), :]
                    )
                    acc = acc + scaled[k] * near
                emit(x0 + i, acc)
            return carry

        lax.fori_loop(0, count // step, body, 0)

    def stage_a(o):
        own(o).wait()
        swap(o).wait_recv()
        send_halos(u, o, h1_s, h1_r)

    def stage_b(o):
        wait_halos(u, o, h1_s, h1_r)

        def emit(x, acc):
            f[o, reach + x, pl.ds(pad, ny), :] = acc

        apply(u, o, emit, 0, planes)
        send_halos(f, o, h2_s, h2_r)

    towers = bands // 2
    tower, core = band // 2, band % 2
    mate = {"dom": dom, "band": tower * 2 + 1 - core}

    def index(k, source):
        own_side = side if k < half else 1 - side
        return source * nb + own_side * half + k % half

    def at_full(k, source, first, count):
        start = pl.multiple_of(index(k, source) * slab + first, 8)
        return full.at[pl.ds(start, count)]

    def at_cells(k, source):
        return cells.at[pl.ds(pl.multiple_of(index(k, source) * share, 8), share)]

    def back(o):
        return remote(
            filt.at[o], at_full(o, band, 0, slab), out_s.at[o], out_r.at[o], partner
        )

    def spread(k, j):
        b = (band + j) % bands
        return remote(
            at_full(k, band, b * share, share), at_cells(k, band),
            gram_s.at[j - 1, k], gram_r.at[j - 1, k], {"dom": dom, "band": b},
        )

    def spread_own(k):
        return pltpu.make_async_copy(
            at_full(k, band, band * share, share), at_cells(k, band), gram_l.at[k]
        )

    def lacking(target_tower, target_core):
        return [((target_tower * 2 + 1 - target_core) * share, share)] + [
            (((target_tower + a) % towers) * 2 * share, 2 * share) for a in range(1, towers)
        ]

    def rest(k, jt):
        return [
            remote(
                at_full(k, band, first, count), at_full(k, band, first, count),
                rest_s.at[jt - 1, k, n], rest_r.at[jt - 1, k, n],
                {"dom": dom, "band": ((tower + jt) % towers) * 2 + core},
            )
            for n, (first, count) in enumerate(lacking((tower + jt) % towers, core))
        ]

    def to_mate(k):
        return [
            remote(
                at_full(k, band, first, count), at_full(k, band, first, count),
                mate_s.at[k, n], mate_r.at[k, n], mate,
            )
            for n, (first, count) in enumerate(lacking(tower, 1 - core))
        ]

    def passing(k, jt):
        source = band - 2 * jt
        return [
            remote(
                at_cells(k, source) if n == 0 else at_full(k, source, first, count),
                at_full(k, source, first, count),
                pass_s.at[jt - 1, k, n], pass_r.at[jt - 1, k, n], mate,
            )
            for n, (first, count) in enumerate(lacking(tower, 1 - core))
        ]

    def start_spread(k):
        for j in range(1, bands):
            spread(k, j).start()
        spread_own(k).start()

        @pl.when(core == 0)
        def _():
            for copy in to_mate(k):
                copy.start()

    def start_rest(k):
        for jt in range(1, towers):
            @pl.when(tower + jt < towers)
            def _():
                for copy in rest(k, jt):
                    copy.start()

    def start_passing(k):
        for jt in range(1, towers):
            spread(k, 2 * jt).wait_recv()
        start_passing_late(k)

    def start_passing_late(k):
        for jt in range(1, towers):
            @pl.when(tower >= jt)
            def _():
                for copy in rest(k, jt):
                    copy.wait_recv()
                for copy in passing(k, jt):
                    copy.start()

    def stage_c(o):
        wait_halos(f, o, h2_s, h2_r)

        def value(x, acc):
            return 2.0 * acc - u[o, reach + x, pl.ds(pad, ny), :]

        def emit_other(x, acc):
            start = pl.multiple_of((x - (1 - side) * nx) * ny, 8)
            filt[o, pl.ds(start, ny), :] = value(x, acc)

        def emit_own(x, acc):
            start = pl.multiple_of(index(o, band) * slab + (x - side * nx) * ny, 8)
            full[pl.ds(start, ny), :] = value(x, acc)

        apply(f, o, emit_other, (1 - side) * nx, nx)
        back(o).start()
        apply(f, o, emit_own, side * nx, nx)
        start_spread(o)

    def stage_x(o):
        back(o).wait_recv()
        start_spread(half + o)

    stage_a(0)
    own_pot.wait()
    swap_pot.wait_recv()
    for j in range(1, bands):
        pass_pot(j).start()
    for j in range(1, bands):
        pass_pot(j).wait_recv()
    stage_b(0)
    waiting = []
    passed = []
    sent = []

    def settle(k):
        waiting.append(k)

    def issue():
        if waiting:
            k = waiting.pop(0)
            start_rest(k)
            sent.append(k)

    for o in range(1, half):
        stage_a(o)
        stage_c(o - 1)
        settle(o - 1)
        if o - 1 < half // 2:
            issue()
        stage_b(o)
    if half > 1:
        stage_x(0)
        settle(half)
    stage_c(half - 1)
    settle(half - 1)
    issue()
    for o in range(1 if half > 1 else 0, half):
        stage_x(o)
        settle(half + o)
        if o == half - 2:
            issue()
        if o < half - 1 and len(passed) < len(sent):
            start_passing(sent[len(passed)])
            passed.append(sent[len(passed)])
    while waiting:
        issue()

    for k in range(nb):
        spread_own(k).wait()
        for j in range(1, bands):
            if j % 2 or k not in passed:
                spread(k, j).wait_recv()

    packed = packed_rows(total, nz)
    chunk = divisor(share, (16, 8))

    def gather(t):
        return jnp.concatenate(
            [cells[pl.ds(t * chunk + i, total, stride=share), :] for i in range(chunk)], axis=1
        )

    def gram_body(t, acc):
        x = gather(t)
        return acc + lax.dot_general(
            x, x, (((1,), (1,)), ((), ())), precision=HIGHEST, preferred_element_type=jnp.float32
        )

    gram = lax.fori_loop(0, share // chunk, gram_body, jnp.zeros((total, total), jnp.float32))
    gram = jnp.concatenate(
        [gram[i * packed:(i + 1) * packed] for i in range(total // packed)], axis=1
    )
    gs[0] = gram
    ar1[me] = gram

    def reduce_1(j):
        return remote(gs.at[0], ar1.at[me], r1_s.at[j - 1], r1_r.at[j - 1], peer_id(j))

    def reduce_2(j):
        return remote(gs.at[1], ar2.at[layer], r2_s.at[j - 1], r2_r.at[j - 1], layer_id(j))

    cells3 = cells.reshape(total, share, nz)
    full3 = full.reshape(total, slab, nz)

    def keep(j):
        b = (band + j) % bands
        at = pl.multiple_of(band * share, 8)
        return pltpu.make_async_copy(
            cells3.at[pl.ds(b * nb, nb)], full3.at[pl.ds(b * nb, nb), pl.ds(at, share)],
            keep_l.at[j - 1],
        )

    for j in range(1, group):
        reduce_1(j).start()
    for j in range(1, bands):
        keep(j).start()
    for k in sent[len(passed):half // 2 + 2]:
        start_passing_late(k)
        passed.append(k)
    for j in range(1, group):
        reduce_1(j).wait_recv()
    part = ar1[0]
    for j in range(1, group):
        part = part + ar1[j]
    gs[1] = part
    ar2[layer] = part
    for j in range(1, layers):
        reduce_2(j).start()
    for j in range(1, layers):
        reduce_2(j).wait_recv()
    work = ar2[0]
    for j in range(1, layers):
        work = work + ar2[j]

    work = jnp.concatenate(
        [work[:, i * total:(i + 1) * total] for i in range(total // packed)], axis=0
    )
    work = jnp.concatenate([work, jnp.zeros((total, total), jnp.float32)], axis=1)
    lane = lax.broadcasted_iota(jnp.int32, work.shape, 1)
    row = lax.broadcasted_iota(jnp.int32, work.shape, 0)
    work = work / jnp.float32(slab * doms * nz)
    work = jnp.where(lane == row + total, jnp.float32(1.0), work)
    for k in range(total):
        root = jnp.sqrt(work[k:k + 1, k:k + 1])
        scale = 1.0 / root
        pivot = work[k:k + 1, :] * scale
        column = work[:, k:k + 1] * scale
        work = jnp.where(row > k, work - column * pivot, jnp.where(row == k, pivot, work))
    solved = jnp.zeros((nb, total), jnp.float32)
    for b in range(bands):
        solved = jnp.where(
            band == b, work[b * nb:(b + 1) * nb, total:2 * total], solved
        )
    for n in range(total):
        for i in range(nb):
            coef[n, i] = jnp.broadcast_to(solved[i:i + 1, n:n + 1], (8, nz))

    for k in sent:
        if k not in passed:
            start_passing_late(k)
    for k in range(nb):
        @pl.when(core == 1)
        def _():
            for copy in to_mate(k):
                copy.wait_recv()

        @pl.when(core == 0)
        def _():
            for copy in to_mate(k):
                copy.wait_send()

        for jt in range(1, towers):
            @pl.when(tower >= jt)
            def _():
                for copy in passing(k, jt):
                    copy.wait()

            @pl.when(tower + jt < towers)
            def _():
                for copy in rest(k, jt):
                    copy.wait_send()

    swap_pot.wait_send()
    for j in range(1, bands):
        pass_pot(j).wait_send()
    for o in range(half):
        swap(o).wait_send()

        @pl.when(has_up)
        def _():
            up(u, o, h1_s, h1_r).wait_send()
            up(f, o, h2_s, h2_r).wait_send()

        @pl.when(has_down)
        def _():
            down(u, o, h1_s, h1_r).wait_send()
            down(f, o, h2_s, h2_r).wait_send()

        back(o).wait_send()
    for k in range(nb):
        for j in range(1, bands):
            spread(k, j).wait_send()
    for j in range(1, group):
        reduce_1(j).wait_send()
    for j in range(1, layers):
        reduce_2(j).wait_send()
    for j in range(1, bands):
        keep(j).wait()


def combine(bands, nb, slab, nz, full, coef, out, held, sem):
    band = lax.axis_index("band")
    tile = 8
    lanes = divisor(slab // tile, (4, 3, 2))
    blocks = slab // (tile * lanes)
    parts = divisor(blocks, (4, 3, 2))
    length = slab // parts

    def copy(part):
        at = pl.ds(part * length, length)
        return pltpu.make_async_copy(held.at[:, at], out.at[:, at], sem.at[part])

    def block(t, carry):
        row = t * (tile * lanes)

        def source(b, acc):
            acc = list(acc)
            for n in range(nb):
                start = pl.multiple_of((b * nb + n) * slab + row, tile)
                values = [full[pl.ds(start + g * tile, tile), :] for g in range(lanes)]
                for i in range(nb):
                    factor = coef[b * nb + n, i]
                    for g in range(lanes):
                        acc[i * lanes + g] = acc[i * lanes + g] + factor * values[g]
            return tuple(acc)

        acc = lax.fori_loop(
            0, band + 1, source, tuple(jnp.zeros((tile, nz), jnp.float32) for _ in range(nb * lanes))
        )
        for i in range(nb):
            for g in range(lanes):
                start = pl.multiple_of(row + g * tile, tile)
                held[i, pl.ds(start, tile), :] = acc[i * lanes + g]
        return carry

    for part in range(parts):
        lax.fori_loop(part * (blocks // parts), (part + 1) * (blocks // parts), block, 0)
        copy(part).start()
    for part in range(parts):
        copy(part).wait()


def shards(doms, bands, orbitals, potential):
    nb, nx, ny, nz = orbitals.shape
    half = nb // 2
    total = nb * bands
    group = 2 * bands
    layers = doms // 2
    slab = nx * ny
    share = slab // bands
    dma = pltpu.SemaphoreType.DMA
    f32 = jnp.float32
    packed = packed_rows(total, nz)
    wide = total * total // packed
    towers = bands // 2
    lacks = max(towers, 1)
    full, coef = pl.pallas_call(
        functools.partial(kernel, doms, bands, nb, nx, ny, nz),
        out_shape=(pltpu.VMEM((total * slab, nz), f32), pltpu.VMEM((total, nb, 8, nz), f32)),
        in_specs=[
            pl.BlockSpec(memory_space=pl.ANY),
            pl.BlockSpec(memory_space=pl.ANY),
        ],
        out_specs=(
            pl.BlockSpec(memory_space=pltpu.VMEM),
            pl.BlockSpec(memory_space=pltpu.VMEM),
        ),
        scratch_shapes=[
            pltpu.VMEM((nz, nz), f32),
            pltpu.VMEM((half, 2 * nx + 2 * reach, ny + 2 * pad, nz), f32),
            pltpu.VMEM((half, 2 * nx + 2 * reach, ny + 2 * pad, nz), f32),
            pltpu.VMEM((half, slab, nz), f32),
            pltpu.VMEM((2 * slab, nz), f32),
            pltpu.VMEM((total * share, nz), f32),
            pltpu.VMEM((2, packed, wide), f32),
            pltpu.VMEM((group, packed, wide), f32),
            pltpu.VMEM((layers, packed, wide), f32),
            dma((half,)),
            dma,
            dma((bands,)),
            dma((bands,)),
            dma((half,)),
            dma((half,)),
            dma((2, half)),
            dma((2, half)),
            dma((2, half)),
            dma((2, half)),
            dma((half,)),
            dma((half,)),
            dma((bands - 1, nb)),
            dma((bands - 1, nb)),
            dma((nb,)),
            dma((max(towers - 1, 1), nb, lacks)),
            dma((max(towers - 1, 1), nb, lacks)),
            dma((max(towers - 1, 1), nb, lacks)),
            dma((max(towers - 1, 1), nb, lacks)),
            dma((nb, lacks)),
            dma((nb, lacks)),
            dma((bands - 1,)),
            dma((group - 1,)),
            dma((group - 1,)),
            dma((max(layers - 1, 1),)),
            dma((max(layers - 1, 1),)),
        ],
        compiler_params=pltpu.CompilerParams(
            collective_id=0, has_side_effects=True, vmem_limit_bytes=48 * 1024 * 1024
        ),
    )(orbitals, potential.reshape(slab, nz))
    parts = 4
    out = pl.pallas_call(
        functools.partial(combine, bands, nb, slab, nz),
        out_shape=jax.ShapeDtypeStruct((nb, slab, nz), f32),
        in_specs=[pl.BlockSpec(memory_space=pltpu.VMEM)] * 2,
        out_specs=pl.BlockSpec(memory_space=pl.ANY),
        scratch_shapes=[pltpu.VMEM((nb, slab, nz), f32), dma((parts,))],
        compiler_params=pltpu.CompilerParams(vmem_limit_bytes=32 * 1024 * 1024),
    )(
        pltpu.with_memory_space_constraint(full, pltpu.VMEM),
        pltpu.with_memory_space_constraint(coef, pltpu.VMEM),
    )
    return out.reshape(orbitals.shape)


def solution(mesh):
    in_specs = (P("band", "dom", None, None), P("dom", None, None))
    out_specs = P("band", "dom", None, None)
    body = functools.partial(shards, mesh.shape["dom"], mesh.shape["band"])
    return jax.shard_map(body, mesh=mesh, in_specs=in_specs, out_specs=out_specs, check_vma=False)
```

```python
import functools
import jax
import jax.numpy as jnp
from jax import lax
from jax.experimental import pallas as pl
from jax.experimental.pallas import tpu as pltpu
from jax.sharding import PartitionSpec as P

stencil_weights = [
    -5369.0 / 1800.0,
    12.0 / 7.0,
    -15.0 / 56.0,
    10.0 / 189.0,
    -1.0 / 112.0,
    2.0 / 1925.0,
    -1.0 / 16632.0,
]
center_shift = 9.5
half_width = 7.5
reach = 6
pad = 8
scaled = [-0.5 * w / half_width for w in stencil_weights]
HIGHEST = lax.Precision.HIGHEST


def divisor(n, options):
    for c in options:
        if n % c == 0:
            return c
    return 1


def packed_rows(total, nz):
    fold = nz // total if total < nz and nz % total == 0 else 1
    return total // fold if total % (8 * fold) == 0 else total


def kernel(
    doms, bands, nb, nx, ny, nz,
    orb, pot, full, coef,
    bz, u, f, filt, potb, cells, gs, ar1, ar2,
    own_sem, pot_sem, pot_s, pot_r, swap_s, swap_r, h1_s, h1_r, h2_s, h2_r,
    out_s, out_r, gram_s, gram_r, gram_l, rest_s, rest_r, pass_s, pass_r, mate_s, mate_r, keep_l,
    r1_s, r1_r, r2_s, r2_r,
):
    half = nb // 2
    planes = 2 * nx
    total = nb * bands
    group = 2 * bands
    slab = nx * ny
    share = slab // bands
    dom = lax.axis_index("dom")
    band = lax.axis_index("band")
    layer = dom // 2
    layers = doms // 2
    side = dom % 2
    base = layer * 2
    me = side * bands + band
    partner = {"dom": base + 1 - side, "band": band}

    def peer(j):
        g = (me + j) % group
        return g // bands, g % bands

    def peer_id(j):
        q, b = peer(j)
        return {"dom": base + q, "band": b}

    def layer_id(j):
        return {"dom": ((layer + j) % layers) * 2 + side, "band": band}

    barrier = pltpu.get_barrier_semaphore()
    for j in range(1, group):
        pl.semaphore_signal(barrier, inc=1, device_id=peer_id(j), device_id_type=pl.DeviceIdType.MESH)
    for j in range(1, layers):
        pl.semaphore_signal(barrier, inc=1, device_id=layer_id(j), device_id_type=pl.DeviceIdType.MESH)
    pl.semaphore_wait(barrier, group - 1 + layers - 1)

    def remote(src, dst, s, r, dev):
        return pltpu.make_async_remote_copy(
            src_ref=src, dst_ref=dst, send_sem=s, recv_sem=r,
            device_id=dev, device_id_type=pl.DeviceIdType.MESH,
        )

    rows = pl.ds(pad, ny)
    mine = pl.ds(reach + side * nx, nx)

    def swap(o):
        return remote(
            orb.at[(1 - side) * half + o], u.at[o, mine, rows], swap_s.at[o], swap_r.at[o], partner
        )

    pot_rows = pl.ds(pl.multiple_of(band * share, 8), share)
    my_pot = pl.ds(pl.multiple_of(side * slab + band * share, 8), share)
    got_pot = pl.ds(pl.multiple_of((1 - side) * slab + band * share, 8), share)
    swap_pot = remote(pot.at[pot_rows], potb.at[my_pot], pot_s.at[0], pot_r.at[0], partner)

    def pass_pot(j):
        return remote(
            potb.at[got_pot], potb.at[got_pot], pot_s.at[j], pot_r.at[j],
            {"dom": dom, "band": (band + j) % bands},
        )

    def own(o):
        return pltpu.make_async_copy(orb.at[side * half + o], u.at[o, mine, rows], own_sem.at[o])

    own_pot = pltpu.make_async_copy(
        pot, potb.at[pl.ds(pl.multiple_of(side * slab, 8), slab)], pot_sem
    )

    swap(0).start()
    swap_pot.start()
    for o in range(1, half):
        swap(o).start()
    for o in range(half):
        own(o).start()
    own_pot.start()

    def up(buf, o, s, r):
        return remote(
            buf.at[o, pl.ds(planes, reach), rows], buf.at[o, pl.ds(0, reach), rows],
            s.at[0, o], r.at[0, o], {"dom": dom + 2, "band": band},
        )

    def down(buf, o, s, r):
        return remote(
            buf.at[o, pl.ds(reach, reach), rows], buf.at[o, pl.ds(planes + reach, reach), rows],
            s.at[1, o], r.at[1, o], {"dom": dom - 2, "band": band},
        )

    has_up = layer < layers - 1
    has_down = layer > 0

    def send_halos(buf, o, s, r):
        @pl.when(has_up)
        def _():
            up(buf, o, s, r).start()

        @pl.when(has_down)
        def _():
            down(buf, o, s, r).start()

    def wait_halos(buf, o, s, r):
        @pl.when(has_down)
        def _():
            up(buf, o, s, r).wait_recv()

        @pl.when(has_up)
        def _():
            down(buf, o, s, r).wait_recv()

    distance = jnp.abs(
        lax.broadcasted_iota(jnp.int32, (nz, nz), 0) - lax.broadcasted_iota(jnp.int32, (nz, nz), 1)
    )
    banded = jnp.zeros((nz, nz), jnp.float32)
    for k in range(1, reach + 1):
        banded = jnp.where(distance == k, jnp.float32(scaled[k]), banded)
    bz[...] = banded
    edge = jnp.zeros((planes + 2 * reach, pad, nz), jnp.float32)
    for buf in (u, f):
        for o in range(half):
            buf[o, :, pl.ds(0, pad), :] = edge
            buf[o, :, pl.ds(pad + ny, pad), :] = edge
    empty = jnp.zeros((reach, ny, nz), jnp.float32)
    for buf in (u, f):
        for o in range(half):
            @pl.when(jnp.logical_not(has_down))
            def _():
                buf[o, pl.ds(0, reach), rows, :] = empty

            @pl.when(jnp.logical_not(has_up))
            def _():
                buf[o, pl.ds(planes + reach, reach), rows, :] = empty

    step = divisor(nx, (4, 3, 2))

    def apply(buf, o, emit, low, count):
        def body(t, carry):
            x0 = low + t * step
            centre = [buf[o, reach + x0 + i, pl.ds(pad, ny), :] for i in range(step)]
            along_z = jnp.dot(
                jnp.concatenate(centre, axis=0), bz[...], precision=HIGHEST,
                preferred_element_type=jnp.float32,
            )
            for i in range(step):
                x = reach + x0 + i
                weight = potb[pl.ds(pl.multiple_of((x0 + i) * ny, 8), ny), :] * (1.0 / half_width) + (
                    3.0 * scaled[0] - center_shift / half_width
                )
                acc = along_z[i * ny:(i + 1) * ny] + weight * centre[i]
                for k in range(1, reach + 1):
                    near = buf[o, x + k, pl.ds(pad, ny), :] + buf[o, x - k, pl.ds(pad, ny), :]
                    near = near + (
                        buf[o, x, pl.ds(pad + k, ny), :] + buf[o, x, pl.ds(pad - k, ny), :]
                    )
                    acc = acc + scaled[k] * near
                emit(x0 + i, acc)
            return carry

        lax.fori_loop(0, count // step, body, 0)

    def stage_a(o):
        own(o).wait()
        swap(o).wait_recv()
        send_halos(u, o, h1_s, h1_r)

    def stage_b(o):
        wait_halos(u, o, h1_s, h1_r)

        def emit(x, acc):
            f[o, reach + x, pl.ds(pad, ny), :] = acc

        apply(u, o, emit, 0, planes)
        send_halos(f, o, h2_s, h2_r)

    towers = bands // 2
    tower, core = band // 2, band % 2
    mate = {"dom": dom, "band": tower * 2 + 1 - core}

    def index(k, source):
        own_side = side if k < half else 1 - side
        return source * nb + own_side * half + k % half

    def at_full(k, source, first, count):
        start = pl.multiple_of(index(k, source) * slab + first, 8)
        return full.at[pl.ds(start, count)]

    def at_cells(k, source):
        return cells.at[pl.ds(pl.multiple_of(index(k, source) * share, 8), share)]

    def back(o):
        return remote(
            filt.at[o], at_full(o, band, 0, slab), out_s.at[o], out_r.at[o], partner
        )

    def spread(k, j):
        b = (band + j) % bands
        return remote(
            at_full(k, band, b * share, share), at_cells(k, band),
            gram_s.at[j - 1, k], gram_r.at[j - 1, k], {"dom": dom, "band": b},
        )

    def spread_own(k):
        return pltpu.make_async_copy(
            at_full(k, band, band * share, share), at_cells(k, band), gram_l.at[k]
        )

    def lacking(target_tower, target_core):
        return [((target_tower * 2 + 1 - target_core) * share, share)] + [
            (((target_tower + a) % towers) * 2 * share, 2 * share) for a in range(1, towers)
        ]

    def rest(k, jt):
        return [
            remote(
                at_full(k, band, first, count), at_full(k, band, first, count),
                rest_s.at[jt - 1, k, n], rest_r.at[jt - 1, k, n],
                {"dom": dom, "band": ((tower + jt) % towers) * 2 + core},
            )
            for n, (first, count) in enumerate(lacking((tower + jt) % towers, core)[1:])
        ]

    def to_mate(k):
        return [
            remote(
                at_full(k, band, first, count), at_full(k, band, first, count),
                mate_s.at[k, n], mate_r.at[k, n], mate,
            )
            for n, (first, count) in enumerate(lacking(tower, 1 - core))
        ]

    def passing(k, jt):
        same, other = band - 2 * jt, (tower - jt) * 2 + 1 - core
        pieces = [(at_cells(k, same), at_full(k, same, band * share, share))]
        pieces.append((at_cells(k, other), at_full(k, other, band * share, share)))
        for first, count in lacking(tower, 1 - core)[1:]:
            pieces.append((at_full(k, same, first, count), at_full(k, same, first, count)))
        return [
            remote(src, dst, pass_s.at[jt - 1, k, n], pass_r.at[jt - 1, k, n], mate)
            for n, (src, dst) in enumerate(pieces)
        ]

    def start_spread(k):
        for j in range(1, bands):
            spread(k, j).start()
        spread_own(k).start()

        @pl.when(core == 0)
        def _():
            for copy in to_mate(k):
                copy.start()

    def start_rest(k):
        for jt in range(1, towers):
            @pl.when(tower + jt < towers)
            def _():
                for copy in rest(k, jt):
                    copy.start()

    def start_passing(k):
        for j in range(1, bands):
            spread(k, j).wait_recv()
        start_passing_late(k)

    def start_passing_late(k):
        for jt in range(1, towers):
            @pl.when(tower >= jt)
            def _():
                for copy in rest(k, jt):
                    copy.wait_recv()
                for copy in passing(k, jt):
                    copy.start()

    def stage_c(o):
        wait_halos(f, o, h2_s, h2_r)

        def value(x, acc):
            return 2.0 * acc - u[o, reach + x, pl.ds(pad, ny), :]

        def emit_other(x, acc):
            start = pl.multiple_of((x - (1 - side) * nx) * ny, 8)
            filt[o, pl.ds(start, ny), :] = value(x, acc)

        def emit_own(x, acc):
            start = pl.multiple_of(index(o, band) * slab + (x - side * nx) * ny, 8)
            full[pl.ds(start, ny), :] = value(x, acc)

        apply(f, o, emit_other, (1 - side) * nx, nx)
        back(o).start()
        apply(f, o, emit_own, side * nx, nx)
        start_spread(o)

    def stage_x(o):
        back(o).wait_recv()
        start_spread(half + o)

    stage_a(0)
    own_pot.wait()
    swap_pot.wait_recv()
    for j in range(1, bands):
        pass_pot(j).start()
    for j in range(1, bands):
        pass_pot(j).wait_recv()
    stage_b(0)
    waiting = []
    passed = []
    sent = []

    def settle(k):
        waiting.append(k)

    def issue():
        if waiting:
            k = waiting.pop(0)
            start_rest(k)
            sent.append(k)

    for o in range(1, half):
        stage_a(o)
        stage_c(o - 1)
        settle(o - 1)
        if o - 1 < half // 2:
            issue()
        stage_b(o)
    if half > 1:
        stage_x(0)
        settle(half)
    stage_c(half - 1)
    settle(half - 1)
    issue()
    for o in range(1 if half > 1 else 0, half):
        stage_x(o)
        settle(half + o)
        if o == half - 2:
            issue()
        if o < half - 1 and len(passed) < len(sent):
            start_passing(sent[len(passed)])
            passed.append(sent[len(passed)])
    while waiting:
        issue()

    for k in range(nb):
        spread_own(k).wait()
        for j in range(1, bands):
            if k not in passed:
                spread(k, j).wait_recv()

    packed = packed_rows(total, nz)
    chunk = divisor(share, (16, 8))

    def gather(t):
        return jnp.concatenate(
            [cells[pl.ds(t * chunk + i, total, stride=share), :] for i in range(chunk)], axis=1
        )

    def gram_body(t, acc):
        x = gather(t)
        return acc + lax.dot_general(
            x, x, (((1,), (1,)), ((), ())), precision=HIGHEST, preferred_element_type=jnp.float32
        )

    gram = lax.fori_loop(0, share // chunk, gram_body, jnp.zeros((total, total), jnp.float32))
    gram = jnp.concatenate(
        [gram[i * packed:(i + 1) * packed] for i in range(total // packed)], axis=1
    )
    gs[0] = gram
    ar1[me] = gram

    def reduce_1(j):
        return remote(gs.at[0], ar1.at[me], r1_s.at[j - 1], r1_r.at[j - 1], peer_id(j))

    def reduce_2(j):
        return remote(gs.at[1], ar2.at[layer], r2_s.at[j - 1], r2_r.at[j - 1], layer_id(j))

    cells3 = cells.reshape(total, share, nz)
    full3 = full.reshape(total, slab, nz)

    def keep(j):
        b = (band + j) % bands
        at = pl.multiple_of(band * share, 8)
        return pltpu.make_async_copy(
            cells3.at[pl.ds(b * nb, nb)], full3.at[pl.ds(b * nb, nb), pl.ds(at, share)],
            keep_l.at[j - 1],
        )

    for j in range(1, group):
        reduce_1(j).start()
    for j in range(1, bands):
        keep(j).start()
    for k in sent[len(passed):half // 2 + 2]:
        start_passing_late(k)
        passed.append(k)
    for j in range(1, group):
        reduce_1(j).wait_recv()
    part = ar1[0]
    for j in range(1, group):
        part = part + ar1[j]
    gs[1] = part
    ar2[layer] = part
    for j in range(1, layers):
        reduce_2(j).start()
    for j in range(1, layers):
        reduce_2(j).wait_recv()
    work = ar2[0]
    for j in range(1, layers):
        work = work + ar2[j]

    work = jnp.concatenate(
        [work[:, i * total:(i + 1) * total] for i in range(total // packed)], axis=0
    )
    work = jnp.concatenate([work, jnp.zeros((total, total), jnp.float32)], axis=1)
    lane = lax.broadcasted_iota(jnp.int32, work.shape, 1)
    row = lax.broadcasted_iota(jnp.int32, work.shape, 0)
    work = work / jnp.float32(slab * doms * nz)
    work = jnp.where(lane == row + total, jnp.float32(1.0), work)
    for k in range(total):
        root = jnp.sqrt(work[k:k + 1, k:k + 1])
        scale = 1.0 / root
        pivot = work[k:k + 1, :] * scale
        column = work[:, k:k + 1] * scale
        work = jnp.where(row > k, work - column * pivot, jnp.where(row == k, pivot, work))
    solved = jnp.zeros((nb, total), jnp.float32)
    for b in range(bands):
        solved = jnp.where(
            band == b, work[b * nb:(b + 1) * nb, total:2 * total], solved
        )
    for n in range(total):
        for i in range(nb):
            coef[n, i] = jnp.broadcast_to(solved[i:i + 1, n:n + 1], (8, nz))

    for k in sent:
        if k not in passed:
            start_passing_late(k)
    for k in range(nb):
        @pl.when(core == 1)
        def _():
            for copy in to_mate(k):
                copy.wait_recv()

        @pl.when(core == 0)
        def _():
            for copy in to_mate(k):
                copy.wait_send()

        for jt in range(1, towers):
            @pl.when(tower >= jt)
            def _():
                for copy in passing(k, jt):
                    copy.wait()

            @pl.when(tower + jt < towers)
            def _():
                for copy in rest(k, jt):
                    copy.wait_send()

    swap_pot.wait_send()
    for j in range(1, bands):
        pass_pot(j).wait_send()
    for o in range(half):
        swap(o).wait_send()

        @pl.when(has_up)
        def _():
            up(u, o, h1_s, h1_r).wait_send()
            up(f, o, h2_s, h2_r).wait_send()

        @pl.when(has_down)
        def _():
            down(u, o, h1_s, h1_r).wait_send()
            down(f, o, h2_s, h2_r).wait_send()

        back(o).wait_send()
    for k in range(nb):
        for j in range(1, bands):
            spread(k, j).wait_send()
    for j in range(1, group):
        reduce_1(j).wait_send()
    for j in range(1, layers):
        reduce_2(j).wait_send()
    for j in range(1, bands):
        keep(j).wait()


def combine(bands, nb, slab, nz, full, coef, out, held, sem):
    band = lax.axis_index("band")
    tile = 8
    lanes = divisor(slab // tile, (4, 3, 2))
    blocks = slab // (tile * lanes)
    parts = divisor(blocks, (4, 3, 2))
    length = slab // parts

    def copy(part):
        at = pl.ds(part * length, length)
        return pltpu.make_async_copy(held.at[:, at], out.at[:, at], sem.at[part])

    def block(t, carry):
        row = t * (tile * lanes)

        def source(b, acc):
            acc = list(acc)
            for n in range(nb):
                start = pl.multiple_of((b * nb + n) * slab + row, tile)
                values = [full[pl.ds(start + g * tile, tile), :] for g in range(lanes)]
                for i in range(nb):
                    factor = coef[b * nb + n, i]
                    for g in range(lanes):
                        acc[i * lanes + g] = acc[i * lanes + g] + factor * values[g]
            return tuple(acc)

        acc = lax.fori_loop(
            0, band + 1, source, tuple(jnp.zeros((tile, nz), jnp.float32) for _ in range(nb * lanes))
        )
        for i in range(nb):
            for g in range(lanes):
                start = pl.multiple_of(row + g * tile, tile)
                held[i, pl.ds(start, tile), :] = acc[i * lanes + g]
        return carry

    for part in range(parts):
        lax.fori_loop(part * (blocks // parts), (part + 1) * (blocks // parts), block, 0)
        copy(part).start()
    for part in range(parts):
        copy(part).wait()


def shards(doms, bands, orbitals, potential):
    nb, nx, ny, nz = orbitals.shape
    half = nb // 2
    total = nb * bands
    group = 2 * bands
    layers = doms // 2
    slab = nx * ny
    share = slab // bands
    dma = pltpu.SemaphoreType.DMA
    f32 = jnp.float32
    packed = packed_rows(total, nz)
    wide = total * total // packed
    towers = bands // 2
    lacks = towers + 1
    full, coef = pl.pallas_call(
        functools.partial(kernel, doms, bands, nb, nx, ny, nz),
        out_shape=(pltpu.VMEM((total * slab, nz), f32), pltpu.VMEM((total, nb, 8, nz), f32)),
        in_specs=[
            pl.BlockSpec(memory_space=pl.ANY),
            pl.BlockSpec(memory_space=pl.ANY),
        ],
        out_specs=(
            pl.BlockSpec(memory_space=pltpu.VMEM),
            pl.BlockSpec(memory_space=pltpu.VMEM),
        ),
        scratch_shapes=[
            pltpu.VMEM((nz, nz), f32),
            pltpu.VMEM((half, 2 * nx + 2 * reach, ny + 2 * pad, nz), f32),
            pltpu.VMEM((half, 2 * nx + 2 * reach, ny + 2 * pad, nz), f32),
            pltpu.VMEM((half, slab, nz), f32),
            pltpu.VMEM((2 * slab, nz), f32),
            pltpu.VMEM((total * share, nz), f32),
            pltpu.VMEM((2, packed, wide), f32),
            pltpu.VMEM((group, packed, wide), f32),
            pltpu.VMEM((layers, packed, wide), f32),
            dma((half,)),
            dma,
            dma((bands,)),
            dma((bands,)),
            dma((half,)),
            dma((half,)),
            dma((2, half)),
            dma((2, half)),
            dma((2, half)),
            dma((2, half)),
            dma((half,)),
            dma((half,)),
            dma((bands - 1, nb)),
            dma((bands - 1, nb)),
            dma((nb,)),
            dma((max(towers - 1, 1), nb, lacks)),
            dma((max(towers - 1, 1), nb, lacks)),
            dma((max(towers - 1, 1), nb, lacks)),
            dma((max(towers - 1, 1), nb, lacks)),
            dma((nb, lacks)),
            dma((nb, lacks)),
            dma((bands - 1,)),
            dma((group - 1,)),
            dma((group - 1,)),
            dma((max(layers - 1, 1),)),
            dma((max(layers - 1, 1),)),
        ],
        compiler_params=pltpu.CompilerParams(
            collective_id=0, has_side_effects=True, vmem_limit_bytes=48 * 1024 * 1024
        ),
    )(orbitals, potential.reshape(slab, nz))
    parts = 4
    out = pl.pallas_call(
        functools.partial(combine, bands, nb, slab, nz),
        out_shape=jax.ShapeDtypeStruct((nb, slab, nz), f32),
        in_specs=[pl.BlockSpec(memory_space=pltpu.VMEM)] * 2,
        out_specs=pl.BlockSpec(memory_space=pl.ANY),
        scratch_shapes=[pltpu.VMEM((nb, slab, nz), f32), dma((parts,))],
        compiler_params=pltpu.CompilerParams(vmem_limit_bytes=32 * 1024 * 1024),
    )(
        pltpu.with_memory_space_constraint(full, pltpu.VMEM),
        pltpu.with_memory_space_constraint(coef, pltpu.VMEM),
    )
    return out.reshape(orbitals.shape)


def solution(mesh):
    in_specs = (P("band", "dom", None, None), P("dom", None, None))
    out_specs = P("band", "dom", None, None)
    body = functools.partial(shards, mesh.shape["dom"], mesh.shape["band"])
    return jax.shard_map(body, mesh=mesh, in_specs=in_specs, out_specs=out_specs, check_vma=False)
```

```python
import functools
import jax
import jax.numpy as jnp
from jax import lax
from jax.experimental import pallas as pl
from jax.experimental.pallas import tpu as pltpu
from jax.sharding import PartitionSpec as P

stencil_weights = [
    -5369.0 / 1800.0,
    12.0 / 7.0,
    -15.0 / 56.0,
    10.0 / 189.0,
    -1.0 / 112.0,
    2.0 / 1925.0,
    -1.0 / 16632.0,
]
center_shift = 9.5
half_width = 7.5
reach = 6
pad = 8
scaled = [-0.5 * w / half_width for w in stencil_weights]
HIGHEST = lax.Precision.HIGHEST


def divisor(n, options):
    for c in options:
        if n % c == 0:
            return c
    return 1


def packed_rows(total, nz):
    fold = nz // total if total < nz and nz % total == 0 else 1
    return total // fold if total % (8 * fold) == 0 else total


def kernel(
    doms, bands, nb, nx, ny, nz,
    orb, pot, out,
    bz, u, f, filt, potb, cells, obuf, gs, ar1, ar2, inv,
    own_sem, pot_sem, pot_s, pot_r, swap_s, swap_r, h1_s, h1_r, h2_s, h2_r,
    a2a_s, a2a_r, a2a_l, r1_s, r1_r, r2_s, r2_r, ret_s, ret_r, ret_l,
):
    half = nb // 2
    planes = 2 * nx
    total = nb * bands
    group = 2 * bands
    slab = nx * ny
    share = slab // bands
    dom = lax.axis_index("dom")
    band = lax.axis_index("band")
    layer = dom // 2
    layers = doms // 2
    side = dom % 2
    base = layer * 2
    me = side * bands + band
    partner = {"dom": base + 1 - side, "band": band}

    def peer(j):
        g = (me + j) % group
        return g // bands, g % bands

    def peer_id(j):
        q, b = peer(j)
        return {"dom": base + q, "band": b}

    def layer_id(j):
        return {"dom": ((layer + j) % layers) * 2 + side, "band": band}

    barrier = pltpu.get_barrier_semaphore()
    for j in range(1, group):
        pl.semaphore_signal(barrier, inc=1, device_id=peer_id(j), device_id_type=pl.DeviceIdType.MESH)
    for j in range(1, layers):
        pl.semaphore_signal(barrier, inc=1, device_id=layer_id(j), device_id_type=pl.DeviceIdType.MESH)
    pl.semaphore_wait(barrier, group - 1 + layers - 1)

    def remote(src, dst, s, r, dev):
        return pltpu.make_async_remote_copy(
            src_ref=src, dst_ref=dst, send_sem=s, recv_sem=r,
            device_id=dev, device_id_type=pl.DeviceIdType.MESH,
        )

    rows = pl.ds(pad, ny)
    mine = pl.ds(reach + side * nx, nx)

    def swap(o):
        return remote(
            orb.at[(1 - side) * half + o], u.at[o, mine, rows], swap_s.at[o], swap_r.at[o], partner
        )

    pot_rows = pl.ds(pl.multiple_of(band * share, 8), share)
    my_pot = pl.ds(pl.multiple_of(side * slab + band * share, 8), share)
    got_pot = pl.ds(pl.multiple_of((1 - side) * slab + band * share, 8), share)
    swap_pot = remote(pot.at[pot_rows], potb.at[my_pot], pot_s.at[0], pot_r.at[0], partner)

    def pass_pot(j):
        return remote(
            potb.at[got_pot], potb.at[got_pot], pot_s.at[j], pot_r.at[j],
            {"dom": dom, "band": (band + j) % bands},
        )

    def own(o):
        return pltpu.make_async_copy(orb.at[side * half + o], u.at[o, mine, rows], own_sem.at[o])

    own_pot = pltpu.make_async_copy(
        pot, potb.at[pl.ds(pl.multiple_of(side * slab, 8), slab)], pot_sem
    )

    swap(0).start()
    swap_pot.start()
    for o in range(1, half):
        swap(o).start()
    for o in range(half):
        own(o).start()
    own_pot.start()

    def up(buf, o, s, r):
        return remote(
            buf.at[o, pl.ds(planes, reach), rows], buf.at[o, pl.ds(0, reach), rows],
            s.at[0, o], r.at[0, o], {"dom": dom + 2, "band": band},
        )

    def down(buf, o, s, r):
        return remote(
            buf.at[o, pl.ds(reach, reach), rows], buf.at[o, pl.ds(planes + reach, reach), rows],
            s.at[1, o], r.at[1, o], {"dom": dom - 2, "band": band},
        )

    has_up = layer < layers - 1
    has_down = layer > 0

    def send_halos(buf, o, s, r):
        @pl.when(has_up)
        def _():
            up(buf, o, s, r).start()

        @pl.when(has_down)
        def _():
            down(buf, o, s, r).start()

    def wait_halos(buf, o, s, r):
        @pl.when(has_down)
        def _():
            up(buf, o, s, r).wait_recv()

        @pl.when(has_up)
        def _():
            down(buf, o, s, r).wait_recv()

    distance = jnp.abs(
        lax.broadcasted_iota(jnp.int32, (nz, nz), 0) - lax.broadcasted_iota(jnp.int32, (nz, nz), 1)
    )
    banded = jnp.zeros((nz, nz), jnp.float32)
    for k in range(1, reach + 1):
        banded = jnp.where(distance == k, jnp.float32(scaled[k]), banded)
    bz[...] = banded
    edge = jnp.zeros((planes + 2 * reach, pad, nz), jnp.float32)
    for buf in (u, f):
        for o in range(half):
            buf[o, :, pl.ds(0, pad), :] = edge
            buf[o, :, pl.ds(pad + ny, pad), :] = edge
    empty = jnp.zeros((reach, ny, nz), jnp.float32)
    for buf in (u, f):
        for o in range(half):
            @pl.when(jnp.logical_not(has_down))
            def _():
                buf[o, pl.ds(0, reach), rows, :] = empty

            @pl.when(jnp.logical_not(has_up))
            def _():
                buf[o, pl.ds(planes + reach, reach), rows, :] = empty

    step = divisor(planes, (4, 3, 2))

    def apply(buf, o, emit):
        def body(t, carry):
            x0 = t * step
            centre = [buf[o, reach + x0 + i, pl.ds(pad, ny), :] for i in range(step)]
            along_z = jnp.dot(
                jnp.concatenate(centre, axis=0), bz[...], precision=HIGHEST,
                preferred_element_type=jnp.float32,
            )
            for i in range(step):
                x = reach + x0 + i
                weight = potb[pl.ds(pl.multiple_of((x0 + i) * ny, 8), ny), :] * (1.0 / half_width) + (
                    3.0 * scaled[0] - center_shift / half_width
                )
                acc = along_z[i * ny:(i + 1) * ny] + weight * centre[i]
                for k in range(1, reach + 1):
                    near = buf[o, x + k, pl.ds(pad, ny), :] + buf[o, x - k, pl.ds(pad, ny), :]
                    near = near + (
                        buf[o, x, pl.ds(pad + k, ny), :] + buf[o, x, pl.ds(pad - k, ny), :]
                    )
                    acc = acc + scaled[k] * near
                emit(x0 + i, acc)
            return carry

        lax.fori_loop(0, planes // step, body, 0)

    def stage_a(o):
        own(o).wait()
        swap(o).wait_recv()
        send_halos(u, o, h1_s, h1_r)

    def stage_b(o):
        wait_halos(u, o, h1_s, h1_r)

        def emit(x, acc):
            f[o, reach + x, pl.ds(pad, ny), :] = acc

        apply(u, o, emit)
        send_halos(f, o, h2_s, h2_r)

    def a2a(o, j):
        q, b = peer(j)
        first = pl.multiple_of(q * slab + b * share, 8)
        to = pl.multiple_of((band * nb + side * half + o) * share, 8)
        return remote(
            filt.at[o, pl.ds(first, share)], cells.at[pl.ds(to, share)],
            a2a_s.at[j - 1, o], a2a_r.at[j - 1, o], peer_id(j),
        )

    def a2a_own(o):
        first = pl.multiple_of(me * share, 8)
        to = pl.multiple_of((band * nb + side * half + o) * share, 8)
        return pltpu.make_async_copy(
            filt.at[o, pl.ds(first, share)], cells.at[pl.ds(to, share)], a2a_l.at[o]
        )

    def stage_c(o):
        wait_halos(f, o, h2_s, h2_r)

        def emit(x, acc):
            start = pl.multiple_of(x * ny, 8)
            filt[o, pl.ds(start, ny), :] = 2.0 * acc - u[o, reach + x, pl.ds(pad, ny), :]

        apply(f, o, emit)
        for j in range(1, group):
            a2a(o, j).start()
        a2a_own(o).start()

    stage_a(0)
    own_pot.wait()
    swap_pot.wait_recv()
    for j in range(1, bands):
        pass_pot(j).start()
    for j in range(1, bands):
        pass_pot(j).wait_recv()
    stage_b(0)
    for o in range(1, half):
        stage_a(o)
        stage_c(o - 1)
        stage_b(o)
    stage_c(half - 1)

    for o in range(half):
        a2a_own(o).wait()
        for j in range(1, group):
            a2a(o, j).wait_recv()

    packed = packed_rows(total, nz)
    chunk = divisor(share, (16, 8))

    def gather(t):
        return jnp.concatenate(
            [cells[pl.ds(t * chunk + i, total, stride=share), :] for i in range(chunk)], axis=1
        )

    def gram_body(t, acc):
        x = gather(t)
        return acc + lax.dot_general(
            x, x, (((1,), (1,)), ((), ())), precision=HIGHEST, preferred_element_type=jnp.float32
        )

    gram = lax.fori_loop(0, share // chunk, gram_body, jnp.zeros((total, total), jnp.float32))
    gram = jnp.concatenate(
        [gram[i * packed:(i + 1) * packed] for i in range(total // packed)], axis=1
    )
    gs[0] = gram
    ar1[me] = gram

    def reduce_1(j):
        return remote(gs.at[0], ar1.at[me], r1_s.at[j - 1], r1_r.at[j - 1], peer_id(j))

    def reduce_2(j):
        return remote(gs.at[1], ar2.at[layer], r2_s.at[j - 1], r2_r.at[j - 1], layer_id(j))

    for j in range(1, group):
        reduce_1(j).start()
    for j in range(1, group):
        reduce_1(j).wait_recv()
    part = ar1[0]
    for j in range(1, group):
        part = part + ar1[j]
    gs[1] = part
    ar2[layer] = part
    for j in range(1, layers):
        reduce_2(j).start()
    for j in range(1, layers):
        reduce_2(j).wait_recv()
    work = ar2[0]
    for j in range(1, layers):
        work = work + ar2[j]

    work = jnp.concatenate(
        [work[:, i * total:(i + 1) * total] for i in range(total // packed)], axis=0
    )
    work = jnp.concatenate([work, jnp.zeros((total, total), jnp.float32)], axis=1)
    lane = lax.broadcasted_iota(jnp.int32, work.shape, 1)
    row = lax.broadcasted_iota(jnp.int32, work.shape, 0)
    work = work / jnp.float32(slab * doms * nz)
    work = jnp.where(lane == row + total, jnp.float32(1.0), work)
    for k in range(total):
        root = jnp.sqrt(work[k:k + 1, k:k + 1])
        scale = 1.0 / root
        pivot = work[k:k + 1, :] * scale
        column = work[:, k:k + 1] * scale
        work = jnp.where(row > k, work - column * pivot, jnp.where(row == k, pivot, work))
    inv[...] = work[:, total:2 * total]

    pieces = divisor(share // chunk, (4, 3, 2))
    piece = share // pieces
    obuf3 = obuf.reshape(total, share, nz)

    def ret(s, j):
        b = (band + j) % bands
        at = pl.multiple_of(band * share + s * piece, 8)
        return remote(
            obuf3.at[pl.ds(b * nb, nb), pl.ds(s * piece, piece)],
            out.at[:, pl.ds(at, piece)],
            ret_s.at[j - 1, s], ret_r.at[j - 1, s], {"dom": dom, "band": b},
        )

    def ret_own(s):
        at = pl.multiple_of(band * share + s * piece, 8)
        return pltpu.make_async_copy(
            obuf3.at[pl.ds(band * nb, nb), pl.ds(s * piece, piece)],
            out.at[:, pl.ds(at, piece)], ret_l.at[s],
        )

    for s in range(pieces):
        def ortho_body(t, carry):
            y = jnp.dot(inv[...], gather(t), precision=HIGHEST, preferred_element_type=jnp.float32)
            for i in range(chunk):
                obuf[pl.ds(t * chunk + i, total, stride=share), :] = y[:, i * nz:(i + 1) * nz]
            return carry

        lax.fori_loop(s * (piece // chunk), (s + 1) * (piece // chunk), ortho_body, 0)
        for j in range(1, bands):
            ret(s, j).start()
        ret_own(s).start()

    swap_pot.wait_send()
    for j in range(1, bands):
        pass_pot(j).wait_send()
    for o in range(half):
        swap(o).wait_send()

        @pl.when(has_up)
        def _():
            up(u, o, h1_s, h1_r).wait_send()
            up(f, o, h2_s, h2_r).wait_send()

        @pl.when(has_down)
        def _():
            down(u, o, h1_s, h1_r).wait_send()
            down(f, o, h2_s, h2_r).wait_send()

        for j in range(1, group):
            a2a(o, j).wait_send()
    for j in range(1, group):
        reduce_1(j).wait_send()
    for j in range(1, layers):
        reduce_2(j).wait_send()
    for s in range(pieces):
        ret_own(s).wait()
        for j in range(1, bands):
            ret(s, j).wait()


def deliver(held, out, sem):
    copy = pltpu.make_async_copy(held, out, sem)
    copy.start()
    copy.wait()


def shards(doms, bands, orbitals, potential):
    nb, nx, ny, nz = orbitals.shape
    half = nb // 2
    total = nb * bands
    group = 2 * bands
    layers = doms // 2
    slab = nx * ny
    share = slab // bands
    dma = pltpu.SemaphoreType.DMA
    f32 = jnp.float32
    packed = packed_rows(total, nz)
    wide = total * total // packed
    pieces = divisor(share // divisor(share, (16, 8)), (4, 3, 2))
    out = pl.pallas_call(
        functools.partial(kernel, doms, bands, nb, nx, ny, nz),
        out_shape=pltpu.VMEM((nb, slab, nz), f32),
        in_specs=[
            pl.BlockSpec(memory_space=pl.ANY),
            pl.BlockSpec(memory_space=pl.ANY),
        ],
        out_specs=pl.BlockSpec(memory_space=pltpu.VMEM),
        scratch_shapes=[
            pltpu.VMEM((nz, nz), f32),
            pltpu.VMEM((half, 2 * nx + 2 * reach, ny + 2 * pad, nz), f32),
            pltpu.VMEM((half, 2 * nx + 2 * reach, ny + 2 * pad, nz), f32),
            pltpu.VMEM((half, 2 * slab, nz), f32),
            pltpu.VMEM((2 * slab, nz), f32),
            pltpu.VMEM((total * share, nz), f32),
            pltpu.VMEM((total * share, nz), f32),
            pltpu.VMEM((2, packed, wide), f32),
            pltpu.VMEM((group, packed, wide), f32),
            pltpu.VMEM((layers, packed, wide), f32),
            pltpu.VMEM((total, total), f32),
            dma((half,)),
            dma,
            dma((bands,)),
            dma((bands,)),
            dma((half,)),
            dma((half,)),
            dma((2, half)),
            dma((2, half)),
            dma((2, half)),
            dma((2, half)),
            dma((group - 1, half)),
            dma((group - 1, half)),
            dma((half,)),
            dma((group - 1,)),
            dma((group - 1,)),
            dma((max(layers - 1, 1),)),
            dma((max(layers - 1, 1),)),
            dma((max(bands - 1, 1), pieces)),
            dma((max(bands - 1, 1), pieces)),
            dma((pieces,)),
        ],
        compiler_params=pltpu.CompilerParams(
            collective_id=0, has_side_effects=True, vmem_limit_bytes=60 * 1024 * 1024
        ),
    )(orbitals, potential.reshape(slab, nz))
    out = pl.pallas_call(
        deliver,
        out_shape=jax.ShapeDtypeStruct((nb, slab, nz), f32),
        in_specs=[pl.BlockSpec(memory_space=pl.ANY)],
        out_specs=pl.BlockSpec(memory_space=pl.ANY),
        scratch_shapes=[dma],
        compiler_params=pltpu.CompilerParams(vmem_limit_bytes=16 * 1024 * 1024),
    )(pltpu.with_memory_space_constraint(out, pltpu.VMEM))
    return out.reshape(orbitals.shape)


def solution(mesh):
    in_specs = (P("band", "dom", None, None), P("dom", None, None))
    out_specs = P("band", "dom", None, None)
    body = functools.partial(shards, mesh.shape["dom"], mesh.shape["band"])
    return jax.shard_map(body, mesh=mesh, in_specs=in_specs, out_specs=out_specs, check_vma=False)
```

```python
import functools
import jax
import jax.numpy as jnp
from jax import lax
from jax.experimental import pallas as pl
from jax.experimental.pallas import tpu as pltpu
from jax.sharding import PartitionSpec as P

stencil_weights = [
    -5369.0 / 1800.0,
    12.0 / 7.0,
    -15.0 / 56.0,
    10.0 / 189.0,
    -1.0 / 112.0,
    2.0 / 1925.0,
    -1.0 / 16632.0,
]
center_shift = 9.5
half_width = 7.5
reach = 6
pad = 8
scaled = [-0.5 * w / half_width for w in stencil_weights]
HIGHEST = lax.Precision.HIGHEST


def divisor(n, options):
    for c in options:
        if n % c == 0:
            return c
    return 1


def packed_rows(total, nz):
    fold = nz // total if total < nz and nz % total == 0 else 1
    return total // fold if total % (8 * fold) == 0 else total


def kernel(
    doms, bands, nb, nx, ny, nz,
    orb, pot, out,
    bz, u, f, filt, potb, cells, obuf, gs, ar1, ar2, inv,
    own_sem, pot_sem, pot_s, pot_r, swap_s, swap_r, h1_s, h1_r, h2_s, h2_r,
    a2a_s, a2a_r, a2a_l, r1_s, r1_r, r2_s, r2_r, ret_s, ret_r, ret_l,
):
    half = nb // 2
    planes = 2 * nx
    total = nb * bands
    group = 2 * bands
    slab = nx * ny
    share = slab // bands
    dom = lax.axis_index("dom")
    band = lax.axis_index("band")
    layer = dom // 2
    layers = doms // 2
    side = dom % 2
    base = layer * 2
    me = side * bands + band
    partner = {"dom": base + 1 - side, "band": band}

    def peer(j):
        g = (me + j) % group
        return g // bands, g % bands

    def peer_id(j):
        q, b = peer(j)
        return {"dom": base + q, "band": b}

    def layer_id(j):
        return {"dom": ((layer + j) % layers) * 2 + side, "band": band}

    barrier = pltpu.get_barrier_semaphore()
    for j in range(1, group):
        pl.semaphore_signal(barrier, inc=1, device_id=peer_id(j), device_id_type=pl.DeviceIdType.MESH)
    for j in range(1, layers):
        pl.semaphore_signal(barrier, inc=1, device_id=layer_id(j), device_id_type=pl.DeviceIdType.MESH)
    pl.semaphore_wait(barrier, group - 1 + layers - 1)

    def remote(src, dst, s, r, dev):
        return pltpu.make_async_remote_copy(
            src_ref=src, dst_ref=dst, send_sem=s, recv_sem=r,
            device_id=dev, device_id_type=pl.DeviceIdType.MESH,
        )

    rows = pl.ds(pad, ny)
    mine = pl.ds(reach + side * nx, nx)

    def swap(o):
        return remote(
            orb.at[(1 - side) * half + o], u.at[o, mine, rows], swap_s.at[o], swap_r.at[o], partner
        )

    pot_rows = pl.ds(pl.multiple_of(band * share, 8), share)
    my_pot = pl.ds(pl.multiple_of(side * slab + band * share, 8), share)
    got_pot = pl.ds(pl.multiple_of((1 - side) * slab + band * share, 8), share)
    swap_pot = remote(pot.at[pot_rows], potb.at[my_pot], pot_s.at[0], pot_r.at[0], partner)

    def pass_pot(j):
        return remote(
            potb.at[got_pot], potb.at[got_pot], pot_s.at[j], pot_r.at[j],
            {"dom": dom, "band": (band + j) % bands},
        )

    def own(o):
        return pltpu.make_async_copy(orb.at[side * half + o], u.at[o, mine, rows], own_sem.at[o])

    own_pot = pltpu.make_async_copy(
        pot, potb.at[pl.ds(pl.multiple_of(side * slab, 8), slab)], pot_sem
    )

    swap(0).start()
    swap_pot.start()
    for o in range(1, half):
        swap(o).start()
    for o in range(half):
        own(o).start()
    own_pot.start()

    def up(buf, o, s, r):
        return remote(
            buf.at[o, pl.ds(planes, reach), rows], buf.at[o, pl.ds(0, reach), rows],
            s.at[0, o], r.at[0, o], {"dom": dom + 2, "band": band},
        )

    def down(buf, o, s, r):
        return remote(
            buf.at[o, pl.ds(reach, reach), rows], buf.at[o, pl.ds(planes + reach, reach), rows],
            s.at[1, o], r.at[1, o], {"dom": dom - 2, "band": band},
        )

    has_up = layer < layers - 1
    has_down = layer > 0

    def send_halos(buf, o, s, r):
        @pl.when(has_up)
        def _():
            up(buf, o, s, r).start()

        @pl.when(has_down)
        def _():
            down(buf, o, s, r).start()

    def wait_halos(buf, o, s, r):
        @pl.when(has_down)
        def _():
            up(buf, o, s, r).wait_recv()

        @pl.when(has_up)
        def _():
            down(buf, o, s, r).wait_recv()

    distance = jnp.abs(
        lax.broadcasted_iota(jnp.int32, (nz, nz), 0) - lax.broadcasted_iota(jnp.int32, (nz, nz), 1)
    )
    banded = jnp.zeros((nz, nz), jnp.float32)
    for k in range(1, reach + 1):
        banded = jnp.where(distance == k, jnp.float32(scaled[k]), banded)
    bz[...] = banded
    edge = jnp.zeros((planes + 2 * reach, pad, nz), jnp.float32)
    for buf in (u, f):
        for o in range(half):
            buf[o, :, pl.ds(0, pad), :] = edge
            buf[o, :, pl.ds(pad + ny, pad), :] = edge
    empty = jnp.zeros((reach, ny, nz), jnp.float32)
    for buf in (u, f):
        for o in range(half):
            @pl.when(jnp.logical_not(has_down))
            def _():
                buf[o, pl.ds(0, reach), rows, :] = empty

            @pl.when(jnp.logical_not(has_up))
            def _():
                buf[o, pl.ds(planes + reach, reach), rows, :] = empty

    step = divisor(planes, (4, 3, 2))

    def apply(buf, o, emit):
        def body(t, carry):
            x0 = t * step
            centre = [buf[o, reach + x0 + i, pl.ds(pad, ny), :] for i in range(step)]
            along_z = jnp.dot(
                jnp.concatenate(centre, axis=0), bz[...], precision=HIGHEST,
                preferred_element_type=jnp.float32,
            )
            for i in range(step):
                x = reach + x0 + i
                weight = potb[pl.ds(pl.multiple_of((x0 + i) * ny, 8), ny), :] * (1.0 / half_width) + (
                    3.0 * scaled[0] - center_shift / half_width
                )
                acc = along_z[i * ny:(i + 1) * ny] + weight * centre[i]
                for k in range(1, reach + 1):
                    near = buf[o, x + k, pl.ds(pad, ny), :] + buf[o, x - k, pl.ds(pad, ny), :]
                    near = near + (
                        buf[o, x, pl.ds(pad + k, ny), :] + buf[o, x, pl.ds(pad - k, ny), :]
                    )
                    acc = acc + scaled[k] * near
                emit(x0 + i, acc)
            return carry

        lax.fori_loop(0, planes // step, body, 0)

    def stage_a(o):
        own(o).wait()
        swap(o).wait_recv()
        send_halos(u, o, h1_s, h1_r)

    def stage_b(o):
        wait_halos(u, o, h1_s, h1_r)

        def emit(x, acc):
            f[o, reach + x, pl.ds(pad, ny), :] = acc

        apply(u, o, emit)
        send_halos(f, o, h2_s, h2_r)

    def a2a(o, j):
        q, b = peer(j)
        first = pl.multiple_of(q * slab + b * share, 8)
        to = pl.multiple_of((band * nb + side * half + o) * share, 8)
        return remote(
            filt.at[o, pl.ds(first, share)], cells.at[pl.ds(to, share)],
            a2a_s.at[j - 1, o], a2a_r.at[j - 1, o], peer_id(j),
        )

    def a2a_own(o):
        first = pl.multiple_of(me * share, 8)
        to = pl.multiple_of((band * nb + side * half + o) * share, 8)
        return pltpu.make_async_copy(
            filt.at[o, pl.ds(first, share)], cells.at[pl.ds(to, share)], a2a_l.at[o]
        )

    def stage_c(o):
        wait_halos(f, o, h2_s, h2_r)

        def emit(x, acc):
            start = pl.multiple_of(x * ny, 8)
            filt[o, pl.ds(start, ny), :] = 2.0 * acc - u[o, reach + x, pl.ds(pad, ny), :]

        apply(f, o, emit)
        for j in range(1, group):
            a2a(o, j).start()
        a2a_own(o).start()

    stage_a(0)
    own_pot.wait()
    swap_pot.wait_recv()
    for j in range(1, bands):
        pass_pot(j).start()
    for j in range(1, bands):
        pass_pot(j).wait_recv()
    stage_b(0)
    for o in range(1, half):
        stage_a(o)
        stage_c(o - 1)
        stage_b(o)
    stage_c(half - 1)

    for o in range(half):
        a2a_own(o).wait()
        for j in range(1, group):
            a2a(o, j).wait_recv()

    packed = packed_rows(total, nz)
    chunk = divisor(share, (16, 8))

    def gather(t):
        return jnp.concatenate(
            [cells[pl.ds(t * chunk + i, total, stride=share), :] for i in range(chunk)], axis=1
        )

    def gram_body(t, acc):
        x = gather(t)
        return acc + lax.dot_general(
            x, x, (((1,), (1,)), ((), ())), precision=HIGHEST, preferred_element_type=jnp.float32
        )

    gram = lax.fori_loop(0, share // chunk, gram_body, jnp.zeros((total, total), jnp.float32))
    gram = jnp.concatenate(
        [gram[i * packed:(i + 1) * packed] for i in range(total // packed)], axis=1
    )
    gs[0] = gram
    ar1[me] = gram

    def reduce_1(j):
        return remote(gs.at[0], ar1.at[me], r1_s.at[j - 1], r1_r.at[j - 1], peer_id(j))

    def reduce_2(j):
        return remote(gs.at[1], ar2.at[layer], r2_s.at[j - 1], r2_r.at[j - 1], layer_id(j))

    for j in range(1, group):
        reduce_1(j).start()
    for j in range(1, group):
        reduce_1(j).wait_recv()
    part = ar1[0]
    for j in range(1, group):
        part = part + ar1[j]
    gs[1] = part
    ar2[layer] = part
    for j in range(1, layers):
        reduce_2(j).start()
    for j in range(1, layers):
        reduce_2(j).wait_recv()
    work = ar2[0]
    for j in range(1, layers):
        work = work + ar2[j]

    work = jnp.concatenate(
        [work[:, i * total:(i + 1) * total] for i in range(total // packed)], axis=0
    )
    work = jnp.concatenate([work, jnp.zeros((total, total), jnp.float32)], axis=1)
    lane = lax.broadcasted_iota(jnp.int32, work.shape, 1)
    row = lax.broadcasted_iota(jnp.int32, work.shape, 0)
    work = work / jnp.float32(slab * doms * nz)
    work = jnp.where(lane == row + total, jnp.float32(1.0), work)
    for k in range(total):
        root = jnp.sqrt(work[k:k + 1, k:k + 1])
        scale = 1.0 / root
        pivot = work[k:k + 1, :] * scale
        column = work[:, k:k + 1] * scale
        work = jnp.where(row > k, work - column * pivot, jnp.where(row == k, pivot, work))
    inv[...] = work[:, total:2 * total]

    pieces = divisor(share // chunk, (6, 4, 3, 2))
    piece = share // pieces
    obuf3 = obuf.reshape(total, share, nz)

    def ret(s, j):
        b = (band + j) % bands
        at = pl.multiple_of(band * share + s * piece, 8)
        return remote(
            obuf3.at[pl.ds(b * nb, nb), pl.ds(s * piece, piece)],
            out.at[:, pl.ds(at, piece)],
            ret_s.at[j - 1, s], ret_r.at[j - 1, s], {"dom": dom, "band": b},
        )

    def ret_own(s):
        at = pl.multiple_of(band * share + s * piece, 8)
        return pltpu.make_async_copy(
            obuf3.at[pl.ds(band * nb, nb), pl.ds(s * piece, piece)],
            out.at[:, pl.ds(at, piece)], ret_l.at[s],
        )

    for s in range(pieces):
        def ortho_body(t, carry):
            y = jnp.dot(inv[...], gather(t), precision=HIGHEST, preferred_element_type=jnp.float32)
            for i in range(chunk):
                obuf[pl.ds(t * chunk + i, total, stride=share), :] = y[:, i * nz:(i + 1) * nz]
            return carry

        lax.fori_loop(s * (piece // chunk), (s + 1) * (piece // chunk), ortho_body, 0)
        for j in range(1, bands):
            ret(s, j).start()
        ret_own(s).start()

    swap_pot.wait_send()
    for j in range(1, bands):
        pass_pot(j).wait_send()
    for o in range(half):
        swap(o).wait_send()

        @pl.when(has_up)
        def _():
            up(u, o, h1_s, h1_r).wait_send()
            up(f, o, h2_s, h2_r).wait_send()

        @pl.when(has_down)
        def _():
            down(u, o, h1_s, h1_r).wait_send()
            down(f, o, h2_s, h2_r).wait_send()

        for j in range(1, group):
            a2a(o, j).wait_send()
    for j in range(1, group):
        reduce_1(j).wait_send()
    for j in range(1, layers):
        reduce_2(j).wait_send()
    for s in range(pieces):
        ret_own(s).wait()
        for j in range(1, bands):
            ret(s, j).wait()


def deliver(held, out, sem):
    copy = pltpu.make_async_copy(held, out, sem)
    copy.start()
    copy.wait()


def shards(doms, bands, orbitals, potential):
    nb, nx, ny, nz = orbitals.shape
    half = nb // 2
    total = nb * bands
    group = 2 * bands
    layers = doms // 2
    slab = nx * ny
    share = slab // bands
    dma = pltpu.SemaphoreType.DMA
    f32 = jnp.float32
    packed = packed_rows(total, nz)
    wide = total * total // packed
    pieces = divisor(share // divisor(share, (16, 8)), (6, 4, 3, 2))
    out = pl.pallas_call(
        functools.partial(kernel, doms, bands, nb, nx, ny, nz),
        out_shape=pltpu.VMEM((nb, slab, nz), f32),
        in_specs=[
            pl.BlockSpec(memory_space=pl.ANY),
            pl.BlockSpec(memory_space=pl.ANY),
        ],
        out_specs=pl.BlockSpec(memory_space=pltpu.VMEM),
        scratch_shapes=[
            pltpu.VMEM((nz, nz), f32),
            pltpu.VMEM((half, 2 * nx + 2 * reach, ny + 2 * pad, nz), f32),
            pltpu.VMEM((half, 2 * nx + 2 * reach, ny + 2 * pad, nz), f32),
            pltpu.VMEM((half, 2 * slab, nz), f32),
            pltpu.VMEM((2 * slab, nz), f32),
            pltpu.VMEM((total * share, nz), f32),
            pltpu.VMEM((total * share, nz), f32),
            pltpu.VMEM((2, packed, wide), f32),
            pltpu.VMEM((group, packed, wide), f32),
            pltpu.VMEM((layers, packed, wide), f32),
            pltpu.VMEM((total, total), f32),
            dma((half,)),
            dma,
            dma((bands,)),
            dma((bands,)),
            dma((half,)),
            dma((half,)),
            dma((2, half)),
            dma((2, half)),
            dma((2, half)),
            dma((2, half)),
            dma((group - 1, half)),
            dma((group - 1, half)),
            dma((half,)),
            dma((group - 1,)),
            dma((group - 1,)),
            dma((max(layers - 1, 1),)),
            dma((max(layers - 1, 1),)),
            dma((max(bands - 1, 1), pieces)),
            dma((max(bands - 1, 1), pieces)),
            dma((pieces,)),
        ],
        compiler_params=pltpu.CompilerParams(
            collective_id=0, has_side_effects=True, vmem_limit_bytes=60 * 1024 * 1024
        ),
    )(orbitals, potential.reshape(slab, nz))
    out = pl.pallas_call(
        deliver,
        out_shape=jax.ShapeDtypeStruct((nb, slab, nz), f32),
        in_specs=[pl.BlockSpec(memory_space=pl.ANY)],
        out_specs=pl.BlockSpec(memory_space=pl.ANY),
        scratch_shapes=[dma],
        compiler_params=pltpu.CompilerParams(vmem_limit_bytes=16 * 1024 * 1024),
    )(pltpu.with_memory_space_constraint(out, pltpu.VMEM))
    return out.reshape(orbitals.shape)


def solution(mesh):
    in_specs = (P("band", "dom", None, None), P("dom", None, None))
    out_specs = P("band", "dom", None, None)
    body = functools.partial(shards, mesh.shape["dom"], mesh.shape["band"])
    return jax.shard_map(body, mesh=mesh, in_specs=in_specs, out_specs=out_specs, check_vma=False)
```
